512 devices in a mesh: dom: 128 (over z, y, core), rhs: 4 (over x).
Axes of the slice: x: 4, y: 4, z: 16, core: 2. Of those that a mesh axis runs over, the one named last changes fastest.
Arguments:
- elem_count: int32 [128], P('dom'), may hold values from 1 to 2, as said below
- face_count: int32 [128], P('dom'), may hold values from 4 to 9, as said below
- bound_slot: int32 [128, 2], P('dom'), may hold values from 2 to 7, as said below
- elem_face: int32 [256, 6], P('dom'), may hold values from 0 to 10, as said below
- density: float32 [256, 768], P('dom'), may hold values from 0.25 to 4
- coupling: bfloat16 [256, 768, 768], P('dom', None, 'rhs'), may hold values from -1 to 2
- ainv: bfloat16 [768, 768], replicated, may hold values from -1 to 3, as said below
- loads: bfloat16 [256, 32, 768], P('dom', 'rhs'), may hold values from -60 to 60
Outputs:
- solution: float32 [1152, 32, 128], P('dom', 'rhs')
- residual: float32 [1152, 32, 128], P('dom', 'rhs')
The draws below stay inside these ranges and needn't reach their ends.
Inputs may be any that keep to these rules, and one draw needn't show every extreme that they name: `elem_count`: some device has 2; the live slots of a device come first. `face_count`: the live face slots of a device come first; some device has 9. `bound_slot`: entry 0 is the slot of the face the device owns at its boundary with the previous device, entry 1 that of the face it owns at its boundary with the next device; the first device's entry 0 face and the last device's entry 1 face are read by no other device. `elem_face`: the six entries of a live element are distinct; every live face slot is named by one or two live elements; dead element slots hold 0. `ainv`: symmetric.
All inputs are finite; a program needn't handle non-finite values.
Results may differ from the reference program's by a relative error of at most 0.01.
Values may be sent and summed in bfloat16 or wider, within the bound.
A program may use at most 64 MiB of HBM per device.

```python
import math
import jax
import jax.numpy as jnp
from jax import lax

FSZ = 128
FLUX = 768
RHS = 32
ELEM_CAP = 2
ITERS = 3
TRACE = 768
FCAP = 9
ELEMS = 256
FACES = 1152
N_DOM = 128


def topology(key):
    base_key = jax.random.fold_in(key, 11)
    key_counts, key_peak, key_order = jax.random.split(base_key, 3)
    position = jnp.arange(N_DOM, dtype=jnp.int32)
    counts = jax.random.randint(key_counts, (N_DOM,), 1, ELEM_CAP + 1, dtype=jnp.int32)
    peak_device = jax.random.randint(key_peak, (), 1, N_DOM - 1, dtype=jnp.int32)
    counts = jnp.where(position == peak_device, ELEM_CAP, counts)
    counts = jnp.where(jnp.abs(position - peak_device) == 1, 1, counts)
    counts = jnp.where(position == 0, ELEM_CAP, counts)
    first_dev = (position == 0).astype(jnp.int32)
    last_dev = (position == N_DOM - 1).astype(jnp.int32)
    face_total = 4 * counts + first_dev + last_dev
    lower_slot = 4 * counts - 2
    upper_slot = 4 * counts - 1
    bound_table = jnp.stack([lower_slot, upper_slot], axis=1).astype(jnp.int32)
    count_col = counts[:, None]
    first_col = first_dev[:, None]
    last_col = last_dev[:, None]
    member = jnp.arange(ELEM_CAP, dtype=jnp.int32)[None, :]
    private_a = jnp.broadcast_to(2 * member, (N_DOM, ELEM_CAP))
    private_b = jnp.broadcast_to(2 * member + 1, (N_DOM, ELEM_CAP))
    lower_a = jnp.where(member > 0, 2 * count_col + 2 * (member - 1), 4 * count_col - 2)
    lower_b = jnp.where(member > 0, 2 * count_col + 2 * (member - 1) + 1, jnp.where(first_col == 1, 4 * count_col, FCAP))
    upper_a = jnp.where(member < count_col - 1, 2 * count_col + 2 * member, 4 * count_col - 1)
    upper_b = jnp.where(member < count_col - 1, 2 * count_col + 2 * member + 1, jnp.where(last_col == 1, 4 * count_col, FCAP + 1))
    face_table = jnp.stack([private_a, private_b, lower_a, lower_b, upper_a, upper_b], axis=2)
    face_table = jnp.where((member < count_col)[:, :, None], face_table, 0)
    scores = jax.random.randint(key_order, (N_DOM, ELEM_CAP, 6), 0, 1 << 20, dtype=jnp.int32) * 8 + jnp.arange(6, dtype=jnp.int32)
    shuffle = jnp.argsort(scores, axis=2)
    face_table = jnp.take_along_axis(face_table, shuffle, axis=2)
    return (counts.astype(jnp.int32), face_total.astype(jnp.int32), bound_table, face_table.reshape(N_DOM * ELEM_CAP, 6).astype(jnp.int32))


def draw_elem_count(key, part):
    return topology(key)[0]


def draw_face_count(key, part):
    return topology(key)[1]


def draw_bound_slot(key, part):
    return topology(key)[2]


def draw_elem_face(key, part):
    return topology(key)[3]


def draw_ainv(key, part):
    sub_key = jax.random.fold_in(key, 23)
    noise = jnp.clip(jax.random.normal(sub_key, (FLUX, FLUX), jnp.float32), -6.0, 6.0)
    center = 1.8
    symmetric = (noise + noise.T) * (0.7 / jnp.sqrt(2.0 * FLUX))
    return (center * jnp.eye(FLUX, dtype=jnp.float32) + symmetric).astype(jnp.bfloat16)


def draw_coupling(key, part):
    sub_key = jax.random.fold_in(key, 29)
    noise = 0.5 * jnp.clip(jax.random.normal(sub_key, (ELEMS, FLUX, TRACE), jnp.float32), -6.0, 6.0)
    identity = jnp.eye(FLUX, TRACE, dtype=jnp.float32)[None, :, :]
    return (identity + noise / jnp.sqrt(1.0 * FLUX)).astype(jnp.bfloat16)


def draw_loads(key, part):
    key_noise, key_cols = jax.random.split(jax.random.fold_in(key, 31))
    rising = jnp.arange(ELEMS, dtype=jnp.float32) / (ELEMS - 1)
    columns = jnp.exp(jax.random.uniform(key_cols, (RHS,), jnp.float32, jnp.log(0.3), jnp.log(3.0)))
    row_scales = jnp.exp(jnp.log(3.0) * rising)
    noise = jnp.clip(jax.random.normal(key_noise, (ELEMS, RHS, FLUX), jnp.float32), -6.0, 6.0)
    return (noise * row_scales[:, None, None] * columns[None, :, None]).astype(jnp.bfloat16)


def block_scale(rng, extent, cuts, smallest, top_value):
    factor_of, own = 1.0, jax.random.fold_in(rng, 6)
    for dim, blocks in cuts:
        heights = jnp.exp(jax.random.uniform(jax.random.fold_in(own, dim), (blocks,), jnp.float32, smallest / len(cuts), top_value / len(cuts)))
        factor_of = factor_of * jnp.repeat(heights, extent[dim] // blocks).reshape([-1 if axis == dim else 1 for axis in range(len(extent))])
    return factor_of


def setup_inputs(seed: int = 0) -> dict:
    key_list = jax.random.split(jax.random.key(seed), 9)
    elem_count = draw_elem_count(jax.random.fold_in(key_list[8], 71), 0)
    face_count = draw_face_count(jax.random.fold_in(key_list[8], 71), 0)
    bound_slot = draw_bound_slot(jax.random.fold_in(key_list[8], 71), 0)
    elem_face = draw_elem_face(jax.random.fold_in(key_list[8], 71), 0)
    density = jnp.clip(jnp.exp(math.log(4.0) - 2.7725887 * jax.random.uniform(key_list[4], (ELEMS, FLUX), jnp.float32) ** block_scale(key_list[4], (ELEMS, FLUX), ((0, 128),), -0.2, 0.2)), 0.25, 4.0)
    coupling = draw_coupling(jax.random.fold_in(key_list[8], 71), 0)
    ainv = draw_ainv(jax.random.fold_in(key_list[8], 71), 0)
    loads = draw_loads(jax.random.fold_in(key_list[8], 71), 0)
    return {"elem_count": elem_count, "face_count": face_count, "bound_slot": bound_slot, "elem_face": elem_face, "density": density, "coupling": coupling, "ainv": ainv, "loads": loads}


FULL_ACCURACY = lax.Precision.HIGHEST

def face_numbers(elem_face, bound_slot):
    element = jnp.arange(ELEMS, dtype=jnp.int32)
    owner_device = element // ELEM_CAP
    prev_upper = jnp.roll(bound_slot[:, 1], 1)
    next_lower = jnp.roll(bound_slot[:, 0], -1)
    base_ids = (owner_device * FCAP)[:, None]
    own_ids = base_ids + elem_face
    from_prev = base_ids - FCAP + prev_upper[owner_device][:, None]
    from_next = base_ids + FCAP + next_lower[owner_device][:, None]
    face_index = jnp.where(elem_face == FCAP, from_prev, jnp.where(elem_face == FCAP + 1, from_next, own_ids))
    return jnp.clip(face_index, 0, FACES - 1).astype(jnp.int32)

def reference(elem_count, face_count, bound_slot, elem_face, density, coupling, ainv, loads):
    scaling = lax.rsqrt(density)

    def condense(element_item):
        row_scale, coupling_one, load_one = element_item
        scaled = (row_scale[:, None] * coupling_one.astype(jnp.float32)).astype(jnp.bfloat16)
        applied = jnp.dot(ainv.astype(jnp.float32), scaled.astype(jnp.float32), preferred_element_type=jnp.float32).astype(jnp.bfloat16)
        schur_one = jnp.dot(scaled.T.astype(jnp.float32), applied.astype(jnp.float32), preferred_element_type=jnp.float32)
        weighted = (row_scale[None, :] * load_one.astype(jnp.float32)).astype(jnp.bfloat16)
        forced = jnp.dot(weighted.astype(jnp.float32), ainv.astype(jnp.float32), preferred_element_type=jnp.float32).astype(jnp.bfloat16)
        driving_one = jnp.dot(forced.astype(jnp.float32), scaled.astype(jnp.float32), preferred_element_type=jnp.float32)
        return (schur_one, driving_one)
    schur_full, driving = lax.map(condense, (scaling, coupling, loads))
    element = jnp.arange(ELEMS, dtype=jnp.int32)
    alive_mask = (element % ELEM_CAP < elem_count[element // ELEM_CAP]).astype(jnp.float32)
    schur_full = schur_full * alive_mask[:, None, None]
    driving = driving * alive_mask[:, None, None]
    face_index = face_numbers(elem_face, bound_slot)
    flat_index = face_index.reshape(-1)
    schur_blocks = schur_full.reshape(ELEMS, 6, FSZ, 6, FSZ)
    diagonal_pick = jnp.arange(6)
    tile_blocks = schur_blocks[:, diagonal_pick, :, diagonal_pick, :]
    tile_blocks = jnp.transpose(tile_blocks, (1, 0, 2, 3)).reshape(ELEMS * 6, FSZ, FSZ)
    diag_blocks = jax.ops.segment_sum(tile_blocks, flat_index, FACES)
    slot_all = jnp.arange(FACES, dtype=jnp.int32)
    face_alive = slot_all % FCAP < face_count[slot_all // FCAP]
    diag_blocks = jnp.where(face_alive[:, None, None], diag_blocks, jnp.eye(FSZ, dtype=jnp.float32)[None])
    factor = jnp.linalg.cholesky(diag_blocks)
    identity_stack = jnp.broadcast_to(jnp.eye(FSZ, dtype=jnp.float32)[None], diag_blocks.shape)
    block_inverse = jax.scipy.linalg.cho_solve((factor, True), identity_stack)
    forcing_blocks = jnp.transpose(driving.reshape(ELEMS, RHS, 6, FSZ), (0, 2, 1, 3)).reshape(ELEMS * 6, RHS, FSZ)
    right_side = jax.ops.segment_sum(forcing_blocks, flat_index, FACES)

    def apply_schur(vector):
        element_local_values = vector[face_index]
        element_out = jnp.einsum('ekalb,elrb->ekra', schur_blocks, element_local_values, precision=FULL_ACCURACY)
        return jax.ops.segment_sum(element_out.reshape(ELEMS * 6, RHS, FSZ), flat_index, FACES)

    def precondition(vector):
        return jnp.einsum('fab,frb->fra', block_inverse, vector, precision=FULL_ACCURACY)

    def column_dot(left, right):
        return lax.optimization_barrier(jnp.sum(left * right, axis=(0, 2)))
    solution = jnp.zeros_like(right_side)
    residual = right_side
    precond_res = precondition(residual)
    search_vector = precond_res
    norm_now = column_dot(residual, precond_res)
    for iteration in range(ITERS):
        image = apply_schur(search_vector)
        step_size = norm_now / column_dot(search_vector, image)
        solution = solution + step_size[None, :, None] * search_vector
        residual = residual - step_size[None, :, None] * image
        precond_res = precondition(residual)
        norm_next = column_dot(residual, precond_res)
        search_vector = precond_res + (norm_next / norm_now)[None, :, None] * search_vector
        norm_now = norm_next
    return (solution, residual)
```

```python
import functools

import jax
import jax.numpy as jnp
from jax import lax
from jax.experimental import pallas as pl
from jax.experimental.pallas import tpu as pltpu
from jax.sharding import PartitionSpec as P

FSZ = 128
NF = 9
TR = 768
NR = 16
PLANE = 8
F32 = jnp.float32
BF16 = jnp.bfloat16
MESH = pl.DeviceIdType.MESH


def parts(v):
    hi = v.astype(BF16).astype(F32)
    return jnp.concatenate([hi, v - hi], axis=0).astype(BF16)


def mm(a, b):
    return jnp.dot(a, b, preferred_element_type=F32)


def face(k):
    return slice(k * FSZ, (k + 1) * FSZ)


def kernel(
    nd, npl,
    ec, fc, bs, ef, dens, cpk, loads, ainv, sol, res,
    craw, cmat, btm, sbc, lrecv, drv, dloc, dpar, dsnd, dnbr, msc, dinv,
    tvec, tnb, rvec, rnb, vbuf, vpar, vnb, vnbr, outb, pay, ra, rb,
    lsem, csend, crecv, lsend, lrecvs, dsend, drecv, tsend, trecv, vsend, vrecv,
    asend, arecv, bsend, brecv,
):
    d = lax.axis_index("dom")
    x = lax.axis_index("rhs")
    e = lax.rem(x, 2)
    h = x // 2
    oe = 1 - e
    partner = 2 * h + oe
    nxt, prv = lax.rem(d + 1, nd), lax.rem(d + nd - 1, nd)
    nz = nd // npl
    zz, jj = d // npl, lax.rem(d, npl)
    me_a = jj * 2 + e

    def dev(dd, xx):
        return {"dom": dd, "rhs": xx}

    own = pltpu.make_async_copy(cpk.at[e], craw.at[x], lsem)
    own.start()

    bar = pltpu.get_barrier_semaphore()

    def hello(dd, xx):
        pl.semaphore_signal(bar, inc=1, device_id=dev(dd, xx), device_id_type=MESH)

    for o in range(1, 4):
        hello(d, lax.rem(x + o, 4))
    for q in range(2):
        hello(nxt, 2 * h + q)
        hello(prv, 2 * h + q)

    def plane_peer(o):
        s = lax.rem(me_a + o, 2 * npl)
        return zz * npl + s // 2, 2 * h + lax.rem(s, 2), s

    def axis_peer(o):
        s = lax.rem(zz + o, nz)
        return s * npl + jj, x, s

    @pl.loop(1, 2 * npl)
    def _(o):
        dd, xx, _s = plane_peer(o)
        hello(dd, xx)

    @pl.loop(1, nz)
    def _(o):
        dd, xx, _s = axis_peer(o)
        hello(dd, xx)

    pl.semaphore_wait(bar, 3 + 4 + 2 * npl - 1 + nz - 1)

    def remote(src, dst, ssem, rsem, dd, xx):
        return pltpu.make_async_remote_copy(
            src_ref=src, dst_ref=dst, send_sem=ssem, recv_sem=rsem,
            device_id=dev(dd, xx), device_id_type=MESH,
        )

    def shard_to(o):
        xx = lax.rem(x + o, 4)
        return remote(cpk.at[lax.rem(xx, 2)], craw.at[x], csend.at[o], crecv.at[x], d, xx)

    def shard_from(s):
        return remote(cpk.at[0], craw.at[s], csend.at[0], crecv.at[s], d, partner)

    order = [lax.rem(partner - x + 4, 4), lax.rem(x - partner + 4, 4), 2]
    for o in order:
        shard_to(o).start()
    lcopy = remote(loads.at[oe], lrecv, lsend, lrecvs, d, partner)
    lcopy.start()

    scal = lax.rsqrt(dens[pl.ds(e, 1), :])
    for k in range(6):
        sbc[face(k), :] = jnp.transpose(jnp.broadcast_to(scal[:, face(k)], (FSZ, FSZ)))

    alive = (e < ec[0]).astype(F32)
    al = [(q < ec[0]).astype(F32) for q in range(2)]
    n0 = [ef[0, k] for k in range(6)]
    n1 = [ef[1, k] for k in range(6)]
    mine = [ef[e, k] for k in range(6)]
    theirs = [ef[oe, k] for k in range(6)]
    lo_slot, up_slot = bs[0, 0], bs[0, 1]
    has_prev = (d > 0).astype(F32)
    has_next = (d < nd - 1).astype(F32)

    def eq(a, b):
        return (a == b).astype(F32)

    to_next = [[eq(mine[k], up_slot) for k in range(6)], [eq(mine[k], NF + 1) for k in range(6)]]
    to_prev = [[eq(mine[k], lo_slot) for k in range(6)], [eq(mine[k], NF) for k in range(6)]]
    same = [[eq(mine[k], theirs[q]) for q in range(6)] for k in range(6)]
    from_prev = [
        [eq(mine[k], NF) * has_prev, eq(mine[k], lo_slot) * has_prev] for k in range(6)
    ]
    from_next = [
        [eq(mine[k], NF + 1) * has_next, eq(mine[k], up_slot) * has_next] for k in range(6)
    ]

    lane = lax.broadcasted_iota(jnp.int32, (TR // 2, FSZ), 1)
    amat = ainv[...]
    own.wait()
    for t in range(2):
        p = lax.rem(h + t, 2)
        if t == 0:
            shard_from(partner).wait_recv()
        else:
            shard_from(2 * p).wait_recv()
            shard_from(2 * p + 1).wait_recv()
        cols = pl.multiple_of(p * 384, 128)
        ev, od = craw.at[2 * p], craw.at[2 * p + 1]
        cmat[:, pl.ds(cols, FSZ)] = (ev[0:TR, :].astype(F32) * sbc[...]).astype(BF16)
        cmat[:, pl.ds(cols + 2 * FSZ, FSZ)] = (od[0:TR, :].astype(F32) * sbc[...]).astype(BF16)
        m0, m1 = ev[TR:, :].astype(F32), od[TR:, :].astype(F32)
        top = jnp.where(lane < 64, m0, m1)
        bot = pltpu.roll(jnp.where(lane < 64, m1, m0), 64, 1)
        half = TR // 2
        cmat[0:half, pl.ds(cols + FSZ, FSZ)] = (top * sbc[0:half, :]).astype(BF16)
        cmat[half:TR, pl.ds(cols + FSZ, FSZ)] = (bot * sbc[half:TR, :]).astype(BF16)
        for k in range(3):
            ck = cmat[:, pl.ds(cols + k * FSZ, FSZ)]
            bt = lax.dot_general(
                ck, amat, (((0,), (0,)), ((), ())), preferred_element_type=F32
            ).astype(BF16)
            btm[pl.ds(cols + k * FSZ, FSZ), :] = bt
            dk = mm(bt, ck) * alive
            dloc[3 * p + k] = 0.5 * (dk + jnp.transpose(dk))

    xl, xr = lax.rem(x + 3, 4), lax.rem(x + 1, 4)
    dcp = [
        remote(dloc.at[0:3], dpar.at[0:3], dsend.at[0], drecv.at[0], d, xl),
        remote(dloc.at[3:6], dpar.at[3:6], dsend.at[1], drecv.at[1], d, xr),
    ]
    for c in dcp:
        c.start()
    for side, table in enumerate((to_next, to_prev)):
        for s in range(2):
            acc = table[s][0] * dloc[0]
            for k in range(1, 6):
                acc += table[s][k] * dloc[k]
            dsnd[side, s * FSZ : (s + 1) * FSZ, :] = acc
        slot = up_slot if side == 0 else lo_slot
        live = (slot < fc[0]).astype(F32)
        dsnd[side, 2 * FSZ :, :] = jnp.full((8, FSZ), 1.0, F32) * live
    for side, dd in enumerate((nxt, prv)):
        for q in range(2):
            c = remote(
                dsnd.at[side], dnbr.at[side, e], dsend.at[2 + 2 * side + q],
                drecv.at[2 + 2 * side + e], dd, 2 * h + q,
            )
            c.start()
            dcp.append(c)

    def send_all(ex, t):
        tvec[ex] = t
        out = [remote(tvec.at[ex], rvec.at[ex], tsend.at[ex, 0], trecv.at[ex, 0], d, partner)]
        out[0].start()
        for side, table in enumerate((to_next, to_prev)):
            for s in range(2):
                acc = table[s][0] * t[:, face(0)]
                for k in range(1, 6):
                    acc += table[s][k] * t[:, face(k)]
                tnb[ex, side, s] = acc
            dd = (nxt, prv)[side]
            for q in range(2):
                c = remote(
                    tnb.at[ex, side], rnb.at[ex, side, e], tsend.at[ex, 1 + 2 * side + q],
                    trecv.at[ex, 1 + 2 * side + e], dd, 2 * h + q,
                )
                c.start()
                out.append(c)
        return out

    def assemble(ex, t, cps):
        for c in cps:
            c.wait_send()
        remote(tvec.at[ex], rvec.at[ex], tsend.at[ex, 0], trecv.at[ex, 0], d, partner).wait_recv()
        for side in range(2):
            for q in range(2):
                remote(
                    tnb.at[ex, side], rnb.at[ex, side, q], tsend.at[ex, 0],
                    trecv.at[ex, 1 + 2 * side + q], d, partner,
                ).wait_recv()
        pv = [rnb[ex, 0, 0, s] + rnb[ex, 0, 1, s] for s in range(2)]
        nv = [rnb[ex, 1, 0, s] + rnb[ex, 1, 1, s] for s in range(2)]
        other = [rvec[ex, :, face(q)] for q in range(6)]
        cols = []
        for k in range(6):
            acc = t[:, face(k)]
            for q in range(6):
                acc += same[k][q] * other[q]
            acc += from_prev[k][0] * pv[0] + from_prev[k][1] * pv[1]
            acc += from_next[k][0] * nv[0] + from_next[k][1] * nv[1]
            cols.append(acc)
        return jnp.concatenate(cols, axis=1)

    lcopy.wait()
    srow = scal
    wgt = [
        (loads[e].astype(F32) * srow).astype(BF16).astype(F32),
        (lrecv[...].astype(F32) * srow).astype(BF16).astype(F32),
    ]
    low = e == 0
    weighted = jnp.concatenate(
        [jnp.where(low, wgt[0], wgt[1]), jnp.where(low, wgt[1], wgt[0])], axis=0
    ).astype(BF16)
    forced = mm(weighted, amat).astype(BF16)
    rloc = mm(forced, cmat[...]) * alive
    drv[...] = rloc
    rcp = send_all(0, rloc)

    for c in dcp:
        c.wait_send()
    remote(dloc.at[0:3], dpar.at[0:3], dsend.at[0], drecv.at[0], d, partner).wait_recv()
    remote(dloc.at[3:6], dpar.at[3:6], dsend.at[0], drecv.at[1], d, partner).wait_recv()
    for side in range(2):
        for q in range(2):
            remote(
                dsnd.at[side], dnbr.at[side, q], dsend.at[0], drecv.at[2 + 2 * side + q], d, partner
            ).wait_recv()
    row = lax.broadcasted_iota(jnp.int32, (FSZ, FSZ), 0)
    col = lax.broadcasted_iota(jnp.int32, (FSZ, FSZ), 1)
    eye = (row == col).astype(F32)
    srows, scols = [], []
    for k in range(6):
        acc = dloc[k]
        for q in range(6):
            acc += same[k][q] * dpar[q]
        for s in range(2):
            at = slice(s * FSZ, (s + 1) * FSZ)
            acc += from_prev[k][s] * (dnbr[0, 0, at, :] + dnbr[0, 1, at, :])
            acc += from_next[k][s] * (dnbr[1, 0, at, :] + dnbr[1, 1, at, :])
        flag = jnp.full((1, FSZ), 1.0, F32) * (mine[k] < fc[0]).astype(F32)
        flag = jnp.where(mine[k] == NF, dnbr[0, 0, 2 * FSZ : 2 * FSZ + 1, :], flag)
        flag = jnp.where(mine[k] == NF + 1, dnbr[1, 0, 2 * FSZ : 2 * FSZ + 1, :], flag)
        acc = jnp.where(flag * alive > 0.5, acc, eye)
        diag = acc * eye
        srow_k = lax.rsqrt(jnp.sum(diag, axis=0, keepdims=True))
        scol_k = lax.rsqrt(jnp.sum(diag, axis=1, keepdims=True))
        srows.append(srow_k)
        scols.append(scol_k)
        msc[k] = acc * srow_k * scol_k

    sub8 = lax.broadcasted_iota(jnp.int32, (8, FSZ), 0)
    lane8 = lax.broadcasted_iota(jnp.int32, (8, FSZ), 1)
    diag8 = (sub8 == lane8).astype(F32)

    def split3(v):
        a1 = v.astype(BF16).astype(F32)
        a2 = (v - a1).astype(BF16).astype(F32)
        return a1, a2, v - a1 - a2

    def sweep(jb, carry):
        base = pl.multiple_of(jb * 8, 8)
        shift = lax.rem(FSZ - base, FSZ)
        panels = [pltpu.roll(msc[k, pl.ds(base, 8), :], shift, 1) for k in range(6)]
        inv = list(panels)
        for i in range(8):
            for k in range(6):
                r = inv[k]
                cb = jnp.broadcast_to(r[:, i : i + 1], (8, FSZ))
                pinv = 1.0 / jnp.broadcast_to(cb[i : i + 1, :], (8, FSZ))
                rb_ = jnp.broadcast_to(r[i : i + 1, :], (8, FSZ))
                rn = jnp.where(lane8 == i, 1.0, rb_) * pinv
                inv[k] = jnp.where(sub8 == i, rn, jnp.where(lane8 == i, 0.0, r) - cb * rn)
        for k in range(6):
            xm = pltpu.roll(panels[k] - diag8, base, 1)
            ym = pltpu.roll(jnp.where(lane8 < 8, diag8 - inv[k], inv[k]), base, 1)
            x1, x2, x3 = split3(xm)
            y1, y2, y3 = split3(ym)
            xs = jnp.concatenate([x1, x1, x2, x2, x1, x3], axis=0).astype(BF16)
            ys = jnp.concatenate([y1, y2, y1, y2, y3, y1], axis=0).astype(BF16)
            upd = lax.dot_general(xs, ys, (((0,), (0,)), ((), ())), preferred_element_type=F32)
            msc[k] = msc[k] - upd
            rows = jnp.where(lane8 < 8, -inv[k], inv[k])
            msc[k, pl.ds(base, 8), :] = pltpu.roll(rows, base, 1)
        return carry

    lax.fori_loop(0, FSZ // 8, sweep, 0)
    for k in range(6):
        di = -(msc[k] * srows[k] * scols[k])
        hi = di.astype(BF16)
        dinv[k, :, 0:FSZ] = hi
        dinv[k, :, FSZ:] = (di - hi.astype(F32)).astype(BF16)

    def precondition(v):
        out = []
        for k in range(6):
            y = mm(parts(v[:, face(k)]), dinv[k])
            y = y[:NR] + y[NR:]
            out.append(y[:, :FSZ] + y[:, FSZ:])
        return jnp.concatenate(out, axis=1)

    def apply_s(v):
        u = mm(parts(v), btm[...])
        u = u[:NR] + u[NR:]
        t = mm(parts(u), cmat[...])
        return (t[:NR] + t[NR:]) * alive

    r0 = assemble(0, rloc, rcp)
    vbuf[3] = r0
    w = precondition(r0)
    vbuf[0] = w
    for i in range(3):
        t = apply_s(w)
        cps = send_all(1 + i, t)
        if i < 2:
            full = assemble(1 + i, t, cps)
            vbuf[4 + i] = full
            w = precondition(full) - w
            vbuf[1 + i] = w

    def fold(v):
        acc = v[:, face(0)]
        for k in range(1, 6):
            acc += v[:, face(k)]
        return acc

    prods = []
    for i in range(3):
        wi = vbuf[i]
        for j in range(3):
            prods.append(fold(wi * tvec[1 + j]))
        prods.append(fold(wi * drv[...]))
    pads = [jnp.zeros((NR, FSZ), F32)] * 4
    for c in range(2):
        stack = jnp.concatenate((prods + pads)[8 * c : 8 * c + 8], axis=0)
        pay[0, c : c + 1, :] = jnp.sum(jnp.transpose(stack), axis=0, keepdims=True)
    ra[me_a] = pay[0]

    def plane_send(o):
        dd, xx, s = plane_peer(o)
        return remote(pay.at[0], ra.at[me_a], asend.at[s], arecv.at[me_a], dd, xx)

    def plane_from(o):
        _dd, _xx, s = plane_peer(o)
        return remote(pay.at[0], ra.at[s], asend.at[s], arecv.at[s], d, partner)

    def axis_send(o):
        dd, xx, s = axis_peer(o)
        return remote(pay.at[1], rb.at[zz], bsend.at[s], brecv.at[zz], dd, xx)

    def axis_from(o):
        _dd, _xx, s = axis_peer(o)
        return remote(pay.at[1], rb.at[s], bsend.at[s], brecv.at[s], d, partner)

    @pl.loop(1, 2 * npl)
    def _(o):
        plane_send(o).start()

    @pl.loop(1, 2 * npl)
    def _(o):
        plane_from(o).wait_recv()

    tot = ra[0]
    for s in range(1, 2 * npl):
        tot = tot + ra[s]
    pay[1] = tot
    rb[zz] = tot

    @pl.loop(1, nz)
    def _(o):
        axis_send(o).start()

    vbuf[6] = assemble(3, t, cps)
    m0 = [sum(eq(n0[k], f) for k in range(6)) * al[0] for f in range(NF + 2)]
    m1 = [sum(eq(n1[k], f) for k in range(6)) * al[1] for f in range(NF + 2)]
    mine_w = [jnp.where(e == 0, al[0], al[1] * (1.0 - m0[f])) for f in range(NF + 2)]
    their_w = [jnp.where(e == 1, al[0], al[1] * (1.0 - m0[f])) for f in range(NF + 2)]
    for side, name in enumerate((NF + 1, NF)):
        for v in range(7):
            acc = jnp.zeros((NR, FSZ), F32)
            for k in range(6):
                acc += (eq(mine[k], name) * mine_w[name]) * vbuf[v, :, face(k)]
            vnb[side, v] = acc
    vcp = [
        remote(
            vbuf.at[:, pl.ds(pl.multiple_of(8 * oe, 8), 8), :], vpar, vsend.at[0], vrecv.at[0],
            d, partner,
        )
    ]
    for side, dd in enumerate((nxt, prv)):
        for q in range(2):
            vcp.append(
                remote(
                    vnb.at[side, :, 8 * q : 8 * q + 8, :], vnbr.at[side, e],
                    vsend.at[1 + 2 * side + q], vrecv.at[1 + 2 * side + e], dd, 2 * h + q,
                )
            )
    for c in vcp:
        c.start()
    for c in vcp:
        c.wait_send()
    remote(vpar, vpar, vsend.at[0], vrecv.at[0], d, partner).wait_recv()
    for side in range(2):
        for q in range(2):
            remote(
                vnb.at[side, :, 0:8, :], vnbr.at[side, q], vsend.at[0],
                vrecv.at[1 + 2 * side + q], d, partner,
            ).wait_recv()
    rows = pl.ds(pl.multiple_of(8 * e, 8), 8)
    for f in range(NF):
        free = 1.0 - jnp.maximum(m0[f], m1[f])
        wp = free * eq(lo_slot, f) * has_prev
        wn = free * eq(up_slot, f) * has_next
        for v in range(7):
            acc = wp * (vnbr[0, 0, v] + vnbr[0, 1, v]) + wn * (vnbr[1, 0, v] + vnbr[1, 1, v])
            for k in range(6):
                acc += (eq(mine[k], f) * mine_w[f]) * vbuf[v, rows, face(k)]
                acc += (eq(theirs[k], f) * their_w[f]) * vpar[v, :, face(k)]
            outb[v, f] = acc

    @pl.loop(1, 2 * npl)
    def _(o):
        plane_send(o).wait_send()

    @pl.loop(1, nz)
    def _(o):
        axis_from(o).wait_recv()

    @pl.loop(1, nz)
    def _(o):
        axis_send(o).wait_send()

    for o in order:
        shard_to(o).wait_send()
    tot = rb[0]
    for s in range(1, nz):
        tot = tot + rb[s]

    def pick(q):
        r = jnp.broadcast_to(tot[q // 8 : q // 8 + 1, :], (8, FSZ))
        at = (q % 8) * NR + 8 * e
        return jnp.sum(jnp.where(lane8 == sub8 + at, r, 0.0), axis=1, keepdims=True)

    g = [[pick(4 * i + j) for j in range(3)] for i in range(3)]
    gr = [pick(4 * i + 3) for i in range(3)]

    zero = jnp.zeros((8, 1), F32)
    pi = [zero + 1.0, zero, zero]
    rho = [zero, zero, zero]
    xc = [zero, zero, zero]
    rz = gr[0]
    for it in range(3):
        psp = zero
        for i in range(it + 1):
            for j in range(it + 1):
                psp += pi[i] * pi[j] * g[i][j]
        alpha = rz / psp
        xc = [xc[i] + alpha * pi[i] for i in range(3)]
        rho = [rho[i] - alpha * pi[i] for i in range(3)]
        if it == 2:
            break
        zc = [1.0 + rho[0], rho[0] + rho[1], rho[1] + rho[2]]
        new = zero
        for i in range(it + 2):
            s = gr[i]
            for j in range(it + 1):
                s += rho[j] * g[i][j]
            new += zc[i] * s
        beta = new / rz
        pi = [zc[i] + beta * pi[i] for i in range(3)]
        rz = new
    xb = [jnp.broadcast_to(c, (8, FSZ)) for c in xc]
    rbc = [jnp.broadcast_to(c, (8, FSZ)) for c in rho]
    for f in range(NF):
        sol[f] = xb[0] * outb[0, f] + xb[1] * outb[1, f] + xb[2] * outb[2, f]
        res[f] = outb[3, f] + rbc[0] * outb[4, f] + rbc[1] * outb[5, f] + rbc[2] * outb[6, f]


def per_device(nd, npl, elem_count, face_count, bound_slot, elem_face, density, coupling, ainv, loads):
    odd = lax.rem(lax.axis_index("rhs"), 2) == 1
    main = jnp.where(odd, coupling[:, :, 64:], coupling[:, :, :128])
    mid = jnp.where(odd, coupling[:, :, :64], coupling[:, :, 128:])
    a, b = mid[:, : TR // 2], mid[:, TR // 2 :]
    mid = jnp.where(odd, jnp.concatenate([b, a], axis=2), jnp.concatenate([a, b], axis=2))
    packed = jnp.concatenate([main, mid], axis=1)

    smem = pl.BlockSpec(memory_space=pltpu.SMEM)
    vmem = pl.BlockSpec(memory_space=pltpu.VMEM)
    hbm = pl.BlockSpec(memory_space=pl.ANY)
    dma = pltpu.SemaphoreType.DMA
    nz = nd // npl
    out = jax.ShapeDtypeStruct((NF, 8, FSZ), F32)
    vm = pltpu.VMEM
    return pl.pallas_call(
        functools.partial(kernel, nd, npl),
        out_shape=(out, out),
        in_specs=[smem, smem, smem, smem, vmem, hbm, vmem, vmem],
        out_specs=(vmem, vmem),
        scratch_shapes=[
            vm((4, 1152, FSZ), BF16),
            vm((TR, TR), BF16),
            vm((TR, TR), BF16),
            vm((TR, FSZ), F32),
            vm((8, TR), BF16),
            vm((NR, TR), F32),
            vm((6, FSZ, FSZ), F32),
            vm((6, FSZ, FSZ), F32),
            vm((2, 2 * FSZ + 8, FSZ), F32),
            vm((2, 2, 2 * FSZ + 8, FSZ), F32),
            vm((6, FSZ, FSZ), F32),
            vm((6, FSZ, 2 * FSZ), BF16),
            vm((4, NR, TR), F32),
            vm((4, 2, 2, NR, FSZ), F32),
            vm((4, NR, TR), F32),
            vm((4, 2, 2, 2, NR, FSZ), F32),
            vm((7, NR, TR), F32),
            vm((7, 8, TR), F32),
            vm((2, 7, NR, FSZ), F32),
            vm((2, 2, 7, 8, FSZ), F32),
            vm((7, NF, 8, FSZ), F32),
            vm((2, 2, FSZ), F32),
            vm((2 * npl, 2, FSZ), F32),
            vm((nz, 2, FSZ), F32),
            dma, dma((4,)), dma((4,)), dma, dma, dma((6,)), dma((6,)),
            dma((4, 5)), dma((4, 5)), dma((5,)), dma((5,)),
            dma((2 * npl,)), dma((2 * npl,)), dma((nz,)), dma((nz,)),
        ],
        compiler_params=pltpu.CompilerParams(
            collective_id=0, has_side_effects=True, vmem_limit_bytes=48 * 1024 * 1024
        ),
        name="condense_cg",
    )(elem_count, face_count, bound_slot, elem_face, density, packed, loads, ainv)


def solution(mesh):
    placed = (
        P("dom"),
        P("dom"),
        P("dom", None),
        P("dom", None),
        P("dom", None),
        P("dom", None, "rhs"),
        P(),
        P("dom", "rhs", None),
    )
    nd = mesh.shape["dom"]
    npl = min(PLANE, nd // 2)
    return jax.shard_map(
        functools.partial(per_device, nd, npl),
        mesh=mesh,
        in_specs=placed,
        out_specs=(P("dom", "rhs", None), P("dom", "rhs", None)),
        check_vma=False,
    )
```

```python
import functools

import jax
import jax.numpy as jnp
from jax import lax
from jax.experimental import pallas as pl
from jax.experimental.pallas import tpu as pltpu
from jax.sharding import PartitionSpec as P

FSZ = 128
NF = 9
TR = 768
NR = 16
PLANE = 8
PK = 72
BL = 16
F32 = jnp.float32
BF16 = jnp.bfloat16
MESH = pl.DeviceIdType.MESH


def parts(v):
    hi = v.astype(BF16).astype(F32)
    return jnp.concatenate([hi, v - hi], axis=0).astype(BF16)


def mm(a, b):
    return jnp.dot(a, b, preferred_element_type=F32)


def face(k):
    return slice(k * FSZ, (k + 1) * FSZ)


def kernel(
    nd, npl,
    ec, fc, bs, ef, dens, coup, loads, ainv, sol, res,
    cin, cpk, amt, craw, cmat, btm, sbc, lrecv, drv, dloc, dpar, dsnd, dnbr, msc, wrow, zrow, dinv,
    tvec, tnb, rvec, rnb, vbuf, vpar, vnb, vnbr, outb, pay, ra, rb,
    near, lsem, csend, crecv, lsend, lrecvs, dsend, drecv, tsend, trecv, vsend, vrecv,
    asend, arecv, bsend, brecv,
):
    d = lax.axis_index("dom")
    x = lax.axis_index("rhs")
    e = lax.rem(x, 2)
    h = x // 2
    oe = 1 - e
    partner = 2 * h + oe
    nxt, prv = lax.rem(d + 1, nd), lax.rem(d + nd - 1, nd)
    nz = nd // npl
    zz, jj = d // npl, lax.rem(d, npl)
    me_a = jj * 2 + e

    def dev(dd, xx):
        return {"dom": dd, "rhs": xx}

    loc = [
        pltpu.make_async_copy(coup.at[oe], cin.at[0], lsem.at[0]),
        pltpu.make_async_copy(coup.at[e], cin.at[1], lsem.at[1]),
        pltpu.make_async_copy(ainv, amt, lsem.at[2]),
    ]
    for c in loc:
        c.start()

    bar = pltpu.get_barrier_semaphore()

    def hello(dd, xx):
        pl.semaphore_signal(bar, inc=1, device_id=dev(dd, xx), device_id_type=MESH)

    for o in range(1, 4):
        hello(d, lax.rem(x + o, 4))
    for q in range(2):
        hello(nxt, 2 * h + q)
        hello(prv, 2 * h + q)

    def plane_peer(o):
        s = lax.rem(me_a + o, 2 * npl)
        return zz * npl + s // 2, 2 * h + lax.rem(s, 2), s

    def axis_peer(o):
        s = lax.rem(zz + o, nz)
        return s * npl + jj, x, s

    @pl.loop(1, 2 * npl)
    def _(o):
        dd, xx, _s = plane_peer(o)
        hello(dd, xx)

    above, below = lax.rem(zz + 1, nz) * npl + jj, lax.rem(zz + nz - 1, nz) * npl + jj
    hello(above, x)
    hello(below, x)

    odd = e
    src = lax.broadcasted_iota(jnp.int32, (192, FSZ), 0)
    dst = lax.broadcasted_iota(jnp.int32, (192, FSZ), 1)
    first_mid = 128 * (1 - odd)

    p_main = (src == dst + 64 * odd).astype(F32).astype(BF16)
    is_mid = (src >= first_mid) & (src < first_mid + 64)
    p_low = (is_mid & (src - first_mid == dst)).astype(F32)
    p_high = (is_mid & (src - first_mid + 64 == dst)).astype(F32)
    o32 = odd.astype(F32)
    p_top = (p_low * (1.0 - o32) + p_high * o32).astype(BF16)
    p_bot = (p_high * (1.0 - o32) + p_low * o32).astype(BF16)

    def pack(raw, out):
        out[0:TR, :] = mm(raw[...], p_main).astype(BF16)
        mid = mm(raw[0 : TR // 2, :], p_top) + mm(raw[TR // 2 :, :], p_bot)
        out[TR:, :] = mid.astype(BF16)

    loc[0].wait()
    pack(cin.at[0], cpk)
    loc[1].wait()
    pack(cin.at[1], craw.at[x])

    pl.semaphore_wait(bar, 3 + 4 + 2 * npl - 1 + 2)

    def remote(src, dst, ssem, rsem, dd, xx):
        return pltpu.make_async_remote_copy(
            src_ref=src, dst_ref=dst, send_sem=ssem, recv_sem=rsem,
            device_id=dev(dd, xx), device_id_type=MESH,
        )

    far = lax.rem(x + 2, 4)
    shards = [
        remote(cpk, craw.at[x], csend.at[0], crecv.at[x], d, partner),
        remote(craw.at[x], craw.at[x], csend.at[2], crecv.at[x], d, far),
        remote(cpk, craw.at[x], csend.at[1], crecv.at[x], d, lax.rem(partner + 2, 4)),
    ]

    def shard_from(s):
        return remote(cpk, craw.at[s], csend.at[0], crecv.at[s], d, partner)

    for c in shards:
        c.start()
    lcopy = remote(loads.at[oe], lrecv, lsend, lrecvs, d, partner)
    lcopy.start()

    for _r in range(nz // 2 - 1):
        pl.semaphore_signal(near.at[0], inc=1, device_id=dev(above, x), device_id_type=MESH)
        pl.semaphore_signal(near.at[1], inc=1, device_id=dev(below, x), device_id_type=MESH)
        pl.semaphore_wait(near.at[0], 1)
        pl.semaphore_wait(near.at[1], 1)

    scal = lax.rsqrt(dens[pl.ds(e, 1), :])
    for k in range(6):
        sbc[face(k), :] = jnp.transpose(jnp.broadcast_to(scal[:, face(k)], (FSZ, FSZ)))

    alive = (e < ec[0]).astype(F32)
    al = [(q < ec[0]).astype(F32) for q in range(2)]
    n0 = [ef[0, k] for k in range(6)]
    n1 = [ef[1, k] for k in range(6)]
    mine = [ef[e, k] for k in range(6)]
    theirs = [ef[oe, k] for k in range(6)]
    lo_slot, up_slot = bs[0, 0], bs[0, 1]
    has_prev = (d > 0).astype(F32)
    has_next = (d < nd - 1).astype(F32)

    def eq(a, b):
        return (a == b).astype(F32)

    to_next = [[eq(mine[k], up_slot) for k in range(6)], [eq(mine[k], NF + 1) for k in range(6)]]
    to_prev = [[eq(mine[k], lo_slot) for k in range(6)], [eq(mine[k], NF) for k in range(6)]]
    same = [[eq(mine[k], theirs[q]) for q in range(6)] for k in range(6)]
    from_prev = [
        [eq(mine[k], NF) * has_prev, eq(mine[k], lo_slot) * has_prev] for k in range(6)
    ]
    from_next = [
        [eq(mine[k], NF + 1) * has_next, eq(mine[k], up_slot) * has_next] for k in range(6)
    ]

    lane = lax.broadcasted_iota(jnp.int32, (TR // 2, FSZ), 1)
    row64 = lax.broadcasted_iota(jnp.int32, (64, FSZ), 0)
    lane64 = lax.broadcasted_iota(jnp.int32, (64, FSZ), 1)
    loc[2].wait()
    amat = amt[...]
    for t in range(2):
        p = lax.rem(h + t, 2)
        if t == 0:
            shard_from(partner).wait_recv()
        else:
            shard_from(2 * p).wait_recv()
            shard_from(2 * p + 1).wait_recv()
        cols = pl.multiple_of(p * 384, 128)
        ev, od = craw.at[2 * p], craw.at[2 * p + 1]
        cmat[:, pl.ds(cols, FSZ)] = (ev[0:TR, :].astype(F32) * sbc[...]).astype(BF16)
        cmat[:, pl.ds(cols + 2 * FSZ, FSZ)] = (od[0:TR, :].astype(F32) * sbc[...]).astype(BF16)
        m0, m1 = ev[TR:, :].astype(F32), od[TR:, :].astype(F32)
        top = jnp.where(lane < 64, m0, m1)
        bot = pltpu.roll(jnp.where(lane < 64, m1, m0), 64, 1)
        half = TR // 2
        cmat[0:half, pl.ds(cols + FSZ, FSZ)] = (top * sbc[0:half, :]).astype(BF16)
        cmat[half:TR, pl.ds(cols + FSZ, FSZ)] = (bot * sbc[half:TR, :]).astype(BF16)
        for k in range(3):
            ck = cmat[:, pl.ds(cols + k * FSZ, FSZ)]
            bt = lax.dot_general(
                ck, amat, (((0,), (0,)), ((), ())), preferred_element_type=F32
            ).astype(BF16)
            btm[pl.ds(cols + k * FSZ, FSZ), :] = bt
            dk = mm(bt, ck) * (0.5 * alive)
            dk = dk + jnp.transpose(dk)
            lower = pltpu.roll(dk[64:, :], 64, 1)
            dloc[3 * p + k, 0:64, :] = jnp.where((lane64 < 64) & (lane64 < row64), lower, dk[:64, :])
            tail = jnp.sum(jnp.where(lane64 == row64 + 64, dk[64:, :], 0.0), axis=0, keepdims=True)
            dloc[3 * p + k, 64:, :] = jnp.broadcast_to(tail, (8, FSZ))

    xl, xr = lax.rem(x + 3, 4), lax.rem(x + 1, 4)
    dcp = [
        remote(dloc.at[0:3], dpar.at[0:3], dsend.at[0], drecv.at[0], d, xl),
        remote(dloc.at[3:6], dpar.at[3:6], dsend.at[1], drecv.at[1], d, xr),
    ]
    for c in dcp:
        c.start()
    for side, table in enumerate((to_next, to_prev)):
        for s in range(2):
            acc = table[s][0] * dloc[0]
            for k in range(1, 6):
                acc += table[s][k] * dloc[k]
            dsnd[side, s * PK : (s + 1) * PK, :] = acc
        slot = up_slot if side == 0 else lo_slot
        live = (slot < fc[0]).astype(F32)
        dsnd[side, 2 * PK :, :] = jnp.full((8, FSZ), 1.0, F32) * live
    for side, dd in enumerate((nxt, prv)):
        for q in range(2):
            c = remote(
                dsnd.at[side], dnbr.at[side, e], dsend.at[2 + 2 * side + q],
                drecv.at[2 + 2 * side + e], dd, 2 * h + q,
            )
            c.start()
            dcp.append(c)

    def send_all(ex, t):
        tvec[ex] = t
        out = [remote(tvec.at[ex], rvec.at[ex], tsend.at[ex, 0], trecv.at[ex, 0], d, partner)]
        out[0].start()
        for side, table in enumerate((to_next, to_prev)):
            for s in range(2):
                acc = table[s][0] * t[:, face(0)]
                for k in range(1, 6):
                    acc += table[s][k] * t[:, face(k)]
                tnb[ex, side, s] = acc
            dd = (nxt, prv)[side]
            for q in range(2):
                c = remote(
                    tnb.at[ex, side], rnb.at[ex, side, e], tsend.at[ex, 1 + 2 * side + q],
                    trecv.at[ex, 1 + 2 * side + e], dd, 2 * h + q,
                )
                c.start()
                out.append(c)
        return out

    def assemble(ex, t, cps):
        for c in cps:
            c.wait_send()
        remote(tvec.at[ex], rvec.at[ex], tsend.at[ex, 0], trecv.at[ex, 0], d, partner).wait_recv()
        for side in range(2):
            for q in range(2):
                remote(
                    tnb.at[ex, side], rnb.at[ex, side, q], tsend.at[ex, 0],
                    trecv.at[ex, 1 + 2 * side + q], d, partner,
                ).wait_recv()
        pv = [rnb[ex, 0, 0, s] + rnb[ex, 0, 1, s] for s in range(2)]
        nv = [rnb[ex, 1, 0, s] + rnb[ex, 1, 1, s] for s in range(2)]
        other = [rvec[ex, :, face(q)] for q in range(6)]
        cols = []
        for k in range(6):
            acc = t[:, face(k)]
            for q in range(6):
                acc += same[k][q] * other[q]
            acc += from_prev[k][0] * pv[0] + from_prev[k][1] * pv[1]
            acc += from_next[k][0] * nv[0] + from_next[k][1] * nv[1]
            cols.append(acc)
        return jnp.concatenate(cols, axis=1)

    lcopy.wait()
    srow = scal
    wgt = [
        (loads[e].astype(F32) * srow).astype(BF16).astype(F32),
        (lrecv[...].astype(F32) * srow).astype(BF16).astype(F32),
    ]
    low = e == 0
    weighted = jnp.concatenate(
        [jnp.where(low, wgt[0], wgt[1]), jnp.where(low, wgt[1], wgt[0])], axis=0
    ).astype(BF16)
    forced = mm(weighted, amat).astype(BF16)
    rloc = mm(forced, cmat[...]) * alive
    drv[...] = rloc
    rcp = send_all(0, rloc)

    for c in dcp:
        c.wait_send()
    remote(dloc.at[0:3], dpar.at[0:3], dsend.at[0], drecv.at[0], d, partner).wait_recv()
    remote(dloc.at[3:6], dpar.at[3:6], dsend.at[0], drecv.at[1], d, partner).wait_recv()
    for side in range(2):
        for q in range(2):
            remote(
                dsnd.at[side], dnbr.at[side, q], dsend.at[0], drecv.at[2 + 2 * side + q], d, partner
            ).wait_recv()
    row = lax.broadcasted_iota(jnp.int32, (FSZ, FSZ), 0)
    col = lax.broadcasted_iota(jnp.int32, (FSZ, FSZ), 1)
    eye = (row == col).astype(F32)
    srows, scols = [], []
    for k in range(6):
        acc = dloc[k]
        for q in range(6):
            acc += same[k][q] * dpar[q]
        for s in range(2):
            at = slice(s * PK, (s + 1) * PK)
            acc += from_prev[k][s] * (dnbr[0, 0, at, :] + dnbr[0, 1, at, :])
            acc += from_next[k][s] * (dnbr[1, 0, at, :] + dnbr[1, 1, at, :])
        flag = jnp.full((1, FSZ), 1.0, F32) * (mine[k] < fc[0]).astype(F32)
        flag = jnp.where(mine[k] == NF, dnbr[0, 0, 2 * PK : 2 * PK + 1, :], flag)
        flag = jnp.where(mine[k] == NF + 1, dnbr[1, 0, 2 * PK : 2 * PK + 1, :], flag)
        body, tail = acc[:64, :], acc[64:65, :]
        keep = jnp.where(lane64 == row64, 0.5, 1.0)
        up = jnp.where(lane64 >= row64, body * keep, 0.0)
        dn = pltpu.roll(jnp.where(lane64 < row64, body, 0.0), 64, 1)
        dn = dn + jnp.where(lane64 == row64 + 64, 0.5 * tail, 0.0)
        half = jnp.concatenate([up, dn], axis=0)
        acc = half + jnp.transpose(half)
        acc = jnp.where(flag * alive > 0.5, acc, eye)
        diag = acc * eye
        srow_k = lax.rsqrt(jnp.sum(diag, axis=0, keepdims=True))
        scol_k = lax.rsqrt(jnp.sum(diag, axis=1, keepdims=True))
        srows.append(srow_k)
        scols.append(scol_k)
        msc[k * FSZ : (k + 1) * FSZ, :] = acc * srow_k * scol_k

    msc[6 * FSZ : 7 * FSZ, :] = eye
    msc[7 * FSZ :, :] = eye
    sub8 = lax.broadcasted_iota(jnp.int32, (8, FSZ), 0)
    lane8 = lax.broadcasted_iota(jnp.int32, (8, FSZ), 1)
    laneb = lax.broadcasted_iota(jnp.int32, (BL, FSZ), 1)
    rowb = lax.broadcasted_iota(jnp.int32, (BL, FSZ), 0)

    def at_lane(r, i):
        return jnp.broadcast_to(r[:, i : i + 1], (8, FSZ))

    def invert8(p):
        p = dict(p)

        def key(a, b):
            return (a, b) if a <= b else (b, a)

        for i in range(8):
            dinv_i = 1.0 / p[i, i]
            old = {a: p[key(a, i)] for a in range(8) if a != i}
            fac = {a: old[a] * dinv_i for a in old}
            for a in old:
                for b in old:
                    if a <= b:
                        p[a, b] = p[a, b] - fac[a] * old[b]
            for a in old:
                p[key(a, i)] = fac[a]
            p[i, i] = -dinv_i
        return {(a, b): p[key(a, b)] for a in range(8) for b in range(8)}

    for base in range(0, FSZ, BL):
        r = [msc[pl.ds(base + i, 8, stride=FSZ), :] for i in range(BL)]
        for lo in range(0, BL, 8):
            at = base + lo
            neg = invert8({
                (a, b): at_lane(r[lo + a], at + b) for a in range(8) for b in range(a, 8)
            })
            inside = (lane8 >= at) & (lane8 < at + 8)
            unit = [(lane8 == at + a).astype(F32) for a in range(8)]
            plain = [jnp.where(inside, -unit[b], r[lo + b]) for b in range(8)]
            y = []
            for a in range(8):
                acc = neg[a, 0] * plain[0]
                for b in range(1, 8):
                    acc += neg[a, b] * plain[b]
                y.append(acc)
            for i in range(lo + 8, BL):
                acc = jnp.where(inside, 0.0, r[i])
                for a in range(8):
                    acc += at_lane(r[i], at + a) * y[a]
                r[i] = acc
            for a in range(8):
                i = lo + a
                wrow[8 * i : 8 * i + 8, :] = r[i] - unit[a]
                zrow[8 * i : 8 * i + 8, :] = jnp.where(inside, unit[a], 0.0) - y[a]
        two = jnp.where(laneb == rowb + base, 2.0, 0.0)
        for k in range(6):
            xm = wrow[pl.ds(k, BL, stride=8), :]
            ym = zrow[pl.ds(k, BL, stride=8), :]
            x1 = xm.astype(BF16)
            x2 = (xm - x1.astype(F32)).astype(BF16)
            y1 = ym.astype(BF16)
            y2 = (ym - y1.astype(F32)).astype(BF16)
            xs = jnp.concatenate([x1, x1, x2], axis=0)
            ys = jnp.concatenate([y1, y2, y1], axis=0)
            upd = lax.dot_general(xs, ys, (((0,), (0,)), ((), ())), preferred_element_type=F32)
            mat = slice(k * FSZ, (k + 1) * FSZ)
            msc[mat, :] = msc[mat, :] - upd
            own_rows = slice(k * FSZ + base, k * FSZ + base + BL)
            msc[own_rows, :] = msc[own_rows, :] - two

    for k in range(6):
        di = -(msc[k * FSZ : (k + 1) * FSZ, :] * srows[k] * scols[k])
        hi = di.astype(BF16)
        dinv[k, :, 0:FSZ] = hi
        dinv[k, :, FSZ:] = (di - hi.astype(F32)).astype(BF16)

    def precondition(v):
        out = []
        for k in range(6):
            y = mm(parts(v[:, face(k)]), dinv[k])
            y = y[:NR] + y[NR:]
            out.append(y[:, :FSZ] + y[:, FSZ:])
        return jnp.concatenate(out, axis=1)

    def apply_s(v):
        u = mm(parts(v), btm[...])
        u = u[:NR] + u[NR:]
        t = mm(parts(u), cmat[...])
        return (t[:NR] + t[NR:]) * alive

    r0 = assemble(0, rloc, rcp)
    vbuf[3] = r0
    w = precondition(r0)
    vbuf[0] = w
    for i in range(3):
        t = apply_s(w)
        cps = send_all(1 + i, t)
        if i < 2:
            full = assemble(1 + i, t, cps)
            vbuf[4 + i] = full
            w = precondition(full) - w
            vbuf[1 + i] = w

    def fold(v):
        acc = v[:, face(0)]
        for k in range(1, 6):
            acc += v[:, face(k)]
        return acc

    prods = []
    for i in range(3):
        wi = vbuf[i]
        for j in range(3):
            prods.append(fold(wi * tvec[1 + j]))
        prods.append(fold(wi * drv[...]))
    pads = [jnp.zeros((NR, FSZ), F32)] * 4
    for c in range(2):
        stack = jnp.concatenate((prods + pads)[8 * c : 8 * c + 8], axis=0)
        pay[0, c : c + 1, :] = jnp.sum(jnp.transpose(stack), axis=0, keepdims=True)
    ra[me_a] = pay[0]

    def plane_send(o):
        dd, xx, s = plane_peer(o)
        return remote(pay.at[0], ra.at[me_a], asend.at[s], arecv.at[me_a], dd, xx)

    def plane_from(o):
        _dd, _xx, s = plane_peer(o)
        return remote(pay.at[0], ra.at[s], asend.at[s], arecv.at[s], d, partner)

    def axis_send(o):
        dd, xx, s = axis_peer(o)
        return remote(pay.at[1], rb.at[zz], bsend.at[s], brecv.at[zz], dd, xx)

    def axis_from(o):
        _dd, _xx, s = axis_peer(o)
        return remote(pay.at[1], rb.at[s], bsend.at[s], brecv.at[s], d, partner)

    @pl.loop(1, 2 * npl)
    def _(o):
        plane_send(o).start()

    @pl.loop(1, 2 * npl)
    def _(o):
        plane_from(o).wait_recv()

    tot = ra[0]
    for s in range(1, 2 * npl):
        tot = tot + ra[s]
    pay[1] = tot
    rb[zz] = tot

    @pl.loop(1, nz)
    def _(o):
        axis_send(o).start()

    vbuf[6] = assemble(3, t, cps)
    m0 = [sum(eq(n0[k], f) for k in range(6)) * al[0] for f in range(NF + 2)]
    m1 = [sum(eq(n1[k], f) for k in range(6)) * al[1] for f in range(NF + 2)]
    mine_w = [jnp.where(e == 0, al[0], al[1] * (1.0 - m0[f])) for f in range(NF + 2)]
    their_w = [jnp.where(e == 1, al[0], al[1] * (1.0 - m0[f])) for f in range(NF + 2)]
    for side, name in enumerate((NF + 1, NF)):
        for v in range(7):
            acc = jnp.zeros((NR, FSZ), F32)
            for k in range(6):
                acc += (eq(mine[k], name) * mine_w[name]) * vbuf[v, :, face(k)]
            vnb[side, v] = acc
    vcp = [
        remote(
            vbuf.at[:, pl.ds(pl.multiple_of(8 * oe, 8), 8), :], vpar, vsend.at[0], vrecv.at[0],
            d, partner,
        )
    ]
    for side, dd in enumerate((nxt, prv)):
        for q in range(2):
            vcp.append(
                remote(
                    vnb.at[side, :, 8 * q : 8 * q + 8, :], vnbr.at[side, e],
                    vsend.at[1 + 2 * side + q], vrecv.at[1 + 2 * side + e], dd, 2 * h + q,
                )
            )
    for c in vcp:
        c.start()
    for c in vcp:
        c.wait_send()
    remote(vpar, vpar, vsend.at[0], vrecv.at[0], d, partner).wait_recv()
    for side in range(2):
        for q in range(2):
            remote(
                vnb.at[side, :, 0:8, :], vnbr.at[side, q], vsend.at[0],
                vrecv.at[1 + 2 * side + q], d, partner,
            ).wait_recv()
    rows = pl.ds(pl.multiple_of(8 * e, 8), 8)
    for f in range(NF):
        free = 1.0 - jnp.maximum(m0[f], m1[f])
        wp = free * eq(lo_slot, f) * has_prev
        wn = free * eq(up_slot, f) * has_next
        for v in range(7):
            acc = wp * (vnbr[0, 0, v] + vnbr[0, 1, v]) + wn * (vnbr[1, 0, v] + vnbr[1, 1, v])
            for k in range(6):
                acc += (eq(mine[k], f) * mine_w[f]) * vbuf[v, rows, face(k)]
                acc += (eq(theirs[k], f) * their_w[f]) * vpar[v, :, face(k)]
            outb[v, f] = acc

    @pl.loop(1, 2 * npl)
    def _(o):
        plane_send(o).wait_send()

    @pl.loop(1, nz)
    def _(o):
        axis_from(o).wait_recv()

    @pl.loop(1, nz)
    def _(o):
        axis_send(o).wait_send()

    for c in shards:
        c.wait_send()
    tot = rb[0]
    for s in range(1, nz):
        tot = tot + rb[s]

    def pick(q):
        r = jnp.broadcast_to(tot[q // 8 : q // 8 + 1, :], (8, FSZ))
        at = (q % 8) * NR + 8 * e
        return jnp.sum(jnp.where(lane8 == sub8 + at, r, 0.0), axis=1, keepdims=True)

    g = [[pick(4 * i + j) for j in range(3)] for i in range(3)]
    gr = [pick(4 * i + 3) for i in range(3)]

    zero = jnp.zeros((8, 1), F32)
    pi = [zero + 1.0, zero, zero]
    rho = [zero, zero, zero]
    xc = [zero, zero, zero]
    rz = gr[0]
    for it in range(3):
        psp = zero
        for i in range(it + 1):
            for j in range(it + 1):
                psp += pi[i] * pi[j] * g[i][j]
        alpha = rz / psp
        xc = [xc[i] + alpha * pi[i] for i in range(3)]
        rho = [rho[i] - alpha * pi[i] for i in range(3)]
        if it == 2:
            break
        zc = [1.0 + rho[0], rho[0] + rho[1], rho[1] + rho[2]]
        new = zero
        for i in range(it + 2):
            s = gr[i]
            for j in range(it + 1):
                s += rho[j] * g[i][j]
            new += zc[i] * s
        beta = new / rz
        pi = [zc[i] + beta * pi[i] for i in range(3)]
        rz = new
    xb = [jnp.broadcast_to(c, (8, FSZ)) for c in xc]
    rbc = [jnp.broadcast_to(c, (8, FSZ)) for c in rho]
    for f in range(NF):
        sol[f] = xb[0] * outb[0, f] + xb[1] * outb[1, f] + xb[2] * outb[2, f]
        res[f] = outb[3, f] + rbc[0] * outb[4, f] + rbc[1] * outb[5, f] + rbc[2] * outb[6, f]


def per_device(nd, npl, elem_count, face_count, bound_slot, elem_face, density, coupling, ainv, loads):
    smem = pl.BlockSpec(memory_space=pltpu.SMEM)
    vmem = pl.BlockSpec(memory_space=pltpu.VMEM)
    hbm = pl.BlockSpec(memory_space=pl.ANY)
    dma = pltpu.SemaphoreType.DMA
    nz = nd // npl
    out = jax.ShapeDtypeStruct((NF, 8, FSZ), F32)
    vm = pltpu.VMEM
    return pl.pallas_call(
        functools.partial(kernel, nd, npl),
        out_shape=(out, out),
        in_specs=[smem, smem, smem, smem, vmem, hbm, vmem, hbm],
        out_specs=(vmem, vmem),
        scratch_shapes=[
            vm((2, TR, 192), BF16),
            vm((1152, FSZ), BF16),
            vm((TR, TR), BF16),
            vm((4, 1152, FSZ), BF16),
            vm((TR, TR), BF16),
            vm((TR, TR), BF16),
            vm((TR, FSZ), F32),
            vm((8, TR), BF16),
            vm((NR, TR), F32),
            vm((6, PK, FSZ), F32),
            vm((6, PK, FSZ), F32),
            vm((2, 2 * PK + 8, FSZ), F32),
            vm((2, 2, 2 * PK + 8, FSZ), F32),
            vm((8 * FSZ, FSZ), F32),
            vm((8 * BL, FSZ), F32),
            vm((8 * BL, FSZ), F32),
            vm((6, FSZ, 2 * FSZ), BF16),
            vm((4, NR, TR), F32),
            vm((4, 2, 2, NR, FSZ), F32),
            vm((4, NR, TR), F32),
            vm((4, 2, 2, 2, NR, FSZ), F32),
            vm((7, NR, TR), F32),
            vm((7, 8, TR), F32),
            vm((2, 7, NR, FSZ), F32),
            vm((2, 2, 7, 8, FSZ), F32),
            vm((7, NF, 8, FSZ), F32),
            vm((2, 2, FSZ), F32),
            vm((2 * npl, 2, FSZ), F32),
            vm((nz, 2, FSZ), F32),
            pltpu.SemaphoreType.REGULAR((2,)),
            dma((3,)), dma((3,)), dma((4,)), dma, dma, dma((6,)), dma((6,)),
            dma((4, 5)), dma((4, 5)), dma((5,)), dma((5,)),
            dma((2 * npl,)), dma((2 * npl,)), dma((nz,)), dma((nz,)),
        ],
        compiler_params=pltpu.CompilerParams(
            collective_id=0, has_side_effects=True, vmem_limit_bytes=48 * 1024 * 1024
        ),
        name="condense_cg",
    )(elem_count, face_count, bound_slot, elem_face, density, coupling, loads, ainv)


def solution(mesh):
    placed = (
        P("dom"),
        P("dom"),
        P("dom", None),
        P("dom", None),
        P("dom", None),
        P("dom", None, "rhs"),
        P(),
        P("dom", "rhs", None),
    )
    nd = mesh.shape["dom"]
    npl = min(PLANE, nd // 2)
    return jax.shard_map(
        functools.partial(per_device, nd, npl),
        mesh=mesh,
        in_specs=placed,
        out_specs=(P("dom", "rhs", None), P("dom", "rhs", None)),
        check_vma=False,
    )
```

```python
import functools

import jax
import jax.numpy as jnp
from jax import lax
from jax.experimental import pallas as pl
from jax.experimental.pallas import tpu as pltpu
from jax.sharding import PartitionSpec as P

FSZ = 128
NF = 9
TR = 768
NR = 16
PLANE = 8
VMEM_ALL = 62 * 1024 * 1024
PK = 72
BL = 16
F32 = jnp.float32
BF16 = jnp.bfloat16
MESH = pl.DeviceIdType.MESH


def parts(v):
    hi = v.astype(BF16).astype(F32)
    return jnp.concatenate([hi, v - hi], axis=0).astype(BF16)


def mm(a, b):
    return jnp.dot(a, b, preferred_element_type=F32)


def mm_t(a, b):
    return lax.dot_general(a, b, (((1,), (1,)), ((), ())), preferred_element_type=F32)


def face(k):
    return slice(k * FSZ, (k + 1) * FSZ)


def kernel(
    nd, npl,
    ec, fc, bs, ef, dens, coup, loads, ainv, sol, res,
    amt, craw, cmat, btm, den, lown, lrecv, dloc, dpar, dsnd, dnbr, msc, wrow, zrow, dinv,
    tvec, tnb, rvec, rnb, vbuf, vpar, vnb, vnbr, outb, pay, ra, rb,
    near, lsem, csend, crecv, lsend, lrecvs, dsend, drecv, tsend, trecv, vsend, vrecv,
    asend, arecv, bsend, brecv,
):
    d = lax.axis_index("dom")
    x = lax.axis_index("rhs")
    e = lax.rem(x, 2)
    h = x // 2
    oe = 1 - e
    partner = 2 * h + oe
    nxt, prv = lax.rem(d + 1, nd), lax.rem(d + nd - 1, nd)
    nz = nd // npl
    zz, jj = d // npl, lax.rem(d, npl)
    me_a = jj * 2 + e

    def dev(dd, xx):
        return {"dom": dd, "rhs": xx}

    def rows_of(s):
        return craw.at[pl.ds(pl.multiple_of(192 * s, 64), 192)]

    loc = [
        pltpu.make_async_copy(dens, den, lsem.at[0]),
        pltpu.make_async_copy(coup.at[e], rows_of(x), lsem.at[1]),
        pltpu.make_async_copy(loads.at[e], lown, lsem.at[2]),
        pltpu.make_async_copy(ainv, amt, lsem.at[3]),
    ]
    for c in loc:
        c.start()

    bar = pltpu.get_barrier_semaphore()

    def hello(dd, xx):
        pl.semaphore_signal(bar, inc=1, device_id=dev(dd, xx), device_id_type=MESH)

    for o in range(1, 4):
        hello(d, lax.rem(x + o, 4))
    for q in range(2):
        hello(nxt, 2 * h + q)
        hello(prv, 2 * h + q)
    beside = lax.rem(partner + 2, 4)
    hello(nxt, beside)
    hello(prv, beside)

    def plane_peer(o):
        s = lax.rem(me_a + o, 2 * npl)
        return zz * npl + s // 2, 2 * h + lax.rem(s, 2), s

    def axis_peer(o):
        s = lax.rem(zz + o, nz)
        return s * npl + jj, x, s

    @pl.loop(1, 2 * npl)
    def _(o):
        dd, xx, _s = plane_peer(o)
        hello(dd, xx)

    above, below = lax.rem(zz + 1, nz) * npl + jj, lax.rem(zz + nz - 1, nz) * npl + jj
    hello(above, x)
    hello(below, x)

    pl.semaphore_wait(bar, 3 + 6 + 2 * npl - 1 + 2)

    def remote(src, dst, ssem, rsem, dd, xx):
        return pltpu.make_async_remote_copy(
            src_ref=src, dst_ref=dst, send_sem=ssem, recv_sem=rsem,
            device_id=dev(dd, xx), device_id_type=MESH,
        )

    far = lax.rem(x + 2, 4)
    shards = [
        remote(coup.at[oe], rows_of(x), csend.at[0], crecv.at[x], d, partner),
        remote(coup.at[e], rows_of(x), csend.at[2], crecv.at[x], d, far),
        remote(coup.at[oe], rows_of(x), csend.at[1], crecv.at[x], d, beside),
    ]

    def shard_from(s):
        return remote(coup.at[0], rows_of(s), csend.at[0], crecv.at[s], d, partner)

    for c in shards:
        c.start()
    lcopy = remote(loads.at[oe], lrecv, lsend, lrecvs, d, partner)
    lcopy.start()

    for _r in range(nz // 2 - 1):
        pl.semaphore_signal(near.at[0], inc=1, device_id=dev(above, x), device_id_type=MESH)
        pl.semaphore_signal(near.at[1], inc=1, device_id=dev(below, x), device_id_type=MESH)
        pl.semaphore_wait(near.at[0], 1)
        pl.semaphore_wait(near.at[1], 1)

    loc[0].wait()
    scal = lax.rsqrt(den[pl.ds(e, 1), :])

    alive = (e < ec[0]).astype(F32)
    al = [(q < ec[0]).astype(F32) for q in range(2)]
    n0 = [ef[0, k] for k in range(6)]
    n1 = [ef[1, k] for k in range(6)]
    mine = [ef[e, k] for k in range(6)]
    theirs = [ef[oe, k] for k in range(6)]
    lo_slot, up_slot = bs[0, 0], bs[0, 1]
    has_prev = (d > 0).astype(F32)
    has_next = (d < nd - 1).astype(F32)

    def eq(a, b):
        return (a == b).astype(F32)

    to_next = [[eq(mine[k], up_slot) for k in range(6)], [eq(mine[k], NF + 1) for k in range(6)]]
    to_prev = [[eq(mine[k], lo_slot) for k in range(6)], [eq(mine[k], NF) for k in range(6)]]
    same = [[eq(mine[k], theirs[q]) for q in range(6)] for k in range(6)]
    from_prev = [
        [eq(mine[k], NF) * has_prev, eq(mine[k], lo_slot) * has_prev] for k in range(6)
    ]
    from_next = [
        [eq(mine[k], NF + 1) * has_next, eq(mine[k], up_slot) * has_next] for k in range(6)
    ]

    row64 = lax.broadcasted_iota(jnp.int32, (64, FSZ), 0)
    lane64 = lax.broadcasted_iota(jnp.int32, (64, FSZ), 1)
    loc[1].wait()
    loc[3].wait()
    amat = amt[...]
    for t in range(2):
        p = lax.rem(h + t, 2)
        if t == 0:
            shard_from(partner).wait_recv()
        else:
            shard_from(2 * p).wait_recv()
            shard_from(2 * p + 1).wait_recv()
        at = pl.multiple_of(p * 384, 128)
        for k in range(3):
            rows = pl.ds(at + k * FSZ, FSZ)
            ck = (craw[rows, :].astype(F32) * scal).astype(BF16)
            cmat[rows, :] = ck
            bt = mm(ck, amat).astype(BF16)
            btm[rows, :] = bt
            dk = mm_t(bt, ck) * (0.5 * alive)
            dk = dk + jnp.transpose(dk)
            lower = pltpu.roll(dk[64:, :], 64, 1)
            dloc[3 * p + k, 0:64, :] = jnp.where((lane64 < 64) & (lane64 < row64), lower, dk[:64, :])
            tail = jnp.sum(jnp.where(lane64 == row64 + 64, dk[64:, :], 0.0), axis=0, keepdims=True)
            dloc[3 * p + k, 64:, :] = jnp.broadcast_to(tail, (8, FSZ))

    xl, xr = lax.rem(x + 3, 4), lax.rem(x + 1, 4)
    dcp = [
        remote(dloc.at[0:3], dpar.at[0:3], dsend.at[0], drecv.at[0], d, xl),
        remote(dloc.at[3:6], dpar.at[3:6], dsend.at[1], drecv.at[1], d, xr),
    ]
    for side, table in enumerate((to_next, to_prev)):
        for s in range(2):
            acc = table[s][0] * dloc[0]
            for k in range(1, 6):
                acc += table[s][k] * dloc[k]
            dsnd[side, s * PK : (s + 1) * PK, :] = acc
        slot = up_slot if side == 0 else lo_slot
        live = (slot < fc[0]).astype(F32)
        dsnd[side, 2 * PK :, :] = jnp.full((8, FSZ), 1.0, F32) * live
    for side, dd in enumerate((nxt, prv)):
        for q, xx in enumerate((x, (partner, beside)[side])):
            c = remote(
                dsnd.at[side], dnbr.at[side, e], dsend.at[2 + 2 * side + q],
                drecv.at[2 + 2 * side + e], dd, xx,
            )
            dcp.append(c)

    for c in dcp[2:] + dcp[:2]:
        c.start()

    def send_all(ex, t):
        tvec[ex] = t
        out = [remote(tvec.at[ex], rvec.at[ex], tsend.at[ex, 0], trecv.at[ex, 0], d, partner)]
        for side, table in enumerate((to_next, to_prev)):
            for s in range(2):
                acc = table[s][0] * t[:, face(0)]
                for k in range(1, 6):
                    acc += table[s][k] * t[:, face(k)]
                tnb[ex, side, s] = acc
            dd = (nxt, prv)[side]
            for q in range(2):
                c = remote(
                    tnb.at[ex, side], rnb.at[ex, side, e], tsend.at[ex, 1 + 2 * side + q],
                    trecv.at[ex, 1 + 2 * side + e], dd, 2 * h + q,
                )
                c.start()
                out.append(c)
        out[0].start()
        return out

    def settle(ex, cps):
        for c in cps:
            c.wait_send()
        remote(tvec.at[ex], rvec.at[ex], tsend.at[ex, 0], trecv.at[ex, 0], d, partner).wait_recv()
        for side in range(2):
            for q in range(2):
                remote(
                    tnb.at[ex, side], rnb.at[ex, side, q], tsend.at[ex, 0],
                    trecv.at[ex, 1 + 2 * side + q], d, partner,
                ).wait_recv()

    def assemble(ex, t, cps):
        settle(ex, cps)
        pv = [rnb[ex, 0, 0, s] + rnb[ex, 0, 1, s] for s in range(2)]
        nv = [rnb[ex, 1, 0, s] + rnb[ex, 1, 1, s] for s in range(2)]
        other = [rvec[ex, :, face(q)] for q in range(6)]
        cols = []
        for k in range(6):
            acc = t[:, face(k)]
            for q in range(6):
                acc += same[k][q] * other[q]
            acc += from_prev[k][0] * pv[0] + from_prev[k][1] * pv[1]
            acc += from_next[k][0] * nv[0] + from_next[k][1] * nv[1]
            cols.append(acc)
        return jnp.concatenate(cols, axis=1)

    lcopy.wait()
    loc[2].wait()
    srow = scal
    wgt = [
        (lown[...].astype(F32) * srow).astype(BF16).astype(F32),
        (lrecv[...].astype(F32) * srow).astype(BF16).astype(F32),
    ]
    low = e == 0
    weighted = jnp.concatenate(
        [jnp.where(low, wgt[0], wgt[1]), jnp.where(low, wgt[1], wgt[0])], axis=0
    ).astype(BF16)
    forced = mm(weighted, amat).astype(BF16)
    rloc = mm_t(forced, cmat[...]) * alive
    rcp = send_all(0, rloc)

    for c in dcp:
        c.wait_send()
    remote(dloc.at[0:3], dpar.at[0:3], dsend.at[0], drecv.at[0], d, partner).wait_recv()
    remote(dloc.at[3:6], dpar.at[3:6], dsend.at[0], drecv.at[1], d, partner).wait_recv()
    for side in range(2):
        for q in range(2):
            remote(
                dsnd.at[side], dnbr.at[side, q], dsend.at[0], drecv.at[2 + 2 * side + q], d, partner
            ).wait_recv()
    row = lax.broadcasted_iota(jnp.int32, (FSZ, FSZ), 0)
    col = lax.broadcasted_iota(jnp.int32, (FSZ, FSZ), 1)
    eye = (row == col).astype(F32)
    srows, scols = [], []
    for k in range(6):
        acc = dloc[k]
        for q in range(6):
            acc += same[k][q] * dpar[q]
        for s in range(2):
            at = slice(s * PK, (s + 1) * PK)
            acc += from_prev[k][s] * (dnbr[0, 0, at, :] + dnbr[0, 1, at, :])
            acc += from_next[k][s] * (dnbr[1, 0, at, :] + dnbr[1, 1, at, :])
        flag = jnp.full((1, FSZ), 1.0, F32) * (mine[k] < fc[0]).astype(F32)
        flag = jnp.where(mine[k] == NF, dnbr[0, 0, 2 * PK : 2 * PK + 1, :], flag)
        flag = jnp.where(mine[k] == NF + 1, dnbr[1, 0, 2 * PK : 2 * PK + 1, :], flag)
        body, tail = acc[:64, :], acc[64:65, :]
        keep = jnp.where(lane64 == row64, 0.5, 1.0)
        up = jnp.where(lane64 >= row64, body * keep, 0.0)
        dn = pltpu.roll(jnp.where(lane64 < row64, body, 0.0), 64, 1)
        dn = dn + jnp.where(lane64 == row64 + 64, 0.5 * tail, 0.0)
        half = jnp.concatenate([up, dn], axis=0)
        acc = half + jnp.transpose(half)
        acc = jnp.where(flag * alive > 0.5, acc, eye)
        diag = acc * eye
        srow_k = lax.rsqrt(jnp.sum(diag, axis=0, keepdims=True))
        scol_k = lax.rsqrt(jnp.sum(diag, axis=1, keepdims=True))
        srows.append(srow_k)
        scols.append(scol_k)
        msc[k * FSZ : (k + 1) * FSZ, :] = acc * srow_k * scol_k

    msc[6 * FSZ : 7 * FSZ, :] = eye
    msc[7 * FSZ :, :] = eye
    sub8 = lax.broadcasted_iota(jnp.int32, (8, FSZ), 0)
    lane8 = lax.broadcasted_iota(jnp.int32, (8, FSZ), 1)
    laneb = lax.broadcasted_iota(jnp.int32, (BL, FSZ), 1)
    rowb = lax.broadcasted_iota(jnp.int32, (BL, FSZ), 0)

    def at_lane(r, i):
        return jnp.broadcast_to(r[:, i : i + 1], (8, FSZ))

    def invert8(p):
        p = dict(p)

        def key(a, b):
            return (a, b) if a <= b else (b, a)

        for i in range(8):
            dinv_i = 1.0 / p[i, i]
            old = {a: p[key(a, i)] for a in range(8) if a != i}
            fac = {a: old[a] * dinv_i for a in old}
            for a in old:
                for b in old:
                    if a <= b:
                        p[a, b] = p[a, b] - fac[a] * old[b]
            for a in old:
                p[key(a, i)] = fac[a]
            p[i, i] = -dinv_i
        return {(a, b): p[key(a, b)] for a in range(8) for b in range(8)}

    for base in range(0, FSZ, BL):
        r = [msc[pl.ds(base + i, 8, stride=FSZ), :] for i in range(BL)]
        for lo in range(0, BL, 8):
            at = base + lo
            neg = invert8({
                (a, b): at_lane(r[lo + a], at + b) for a in range(8) for b in range(a, 8)
            })
            inside = (lane8 >= at) & (lane8 < at + 8)
            unit = [(lane8 == at + a).astype(F32) for a in range(8)]
            plain = [jnp.where(inside, -unit[b], r[lo + b]) for b in range(8)]
            y = []
            for a in range(8):
                acc = neg[a, 0] * plain[0]
                for b in range(1, 8):
                    acc += neg[a, b] * plain[b]
                y.append(acc)
            for i in range(lo + 8, BL):
                acc = jnp.where(inside, 0.0, r[i])
                for a in range(8):
                    acc += at_lane(r[i], at + a) * y[a]
                r[i] = acc
            for a in range(8):
                i = lo + a
                wrow[8 * i : 8 * i + 8, :] = r[i] - unit[a]
                zrow[8 * i : 8 * i + 8, :] = jnp.where(inside, unit[a], 0.0) - y[a]
        two = jnp.where(laneb == rowb + base, 2.0, 0.0)
        for k in range(6):
            xm = wrow[pl.ds(k, BL, stride=8), :]
            ym = zrow[pl.ds(k, BL, stride=8), :]
            x1 = xm.astype(BF16)
            x2 = (xm - x1.astype(F32)).astype(BF16)
            y1 = ym.astype(BF16)
            y2 = (ym - y1.astype(F32)).astype(BF16)
            xs = jnp.concatenate([x1, x1, x2], axis=0)
            ys = jnp.concatenate([y1, y2, y1], axis=0)
            upd = lax.dot_general(xs, ys, (((0,), (0,)), ((), ())), preferred_element_type=F32)
            mat = slice(k * FSZ, (k + 1) * FSZ)
            msc[mat, :] = msc[mat, :] - upd
            own_rows = slice(k * FSZ + base, k * FSZ + base + BL)
            msc[own_rows, :] = msc[own_rows, :] - two

    for k in range(6):
        di = -(msc[k * FSZ : (k + 1) * FSZ, :] * srows[k] * scols[k])
        hi = di.astype(BF16)
        dinv[k, :, 0:FSZ] = hi
        dinv[k, :, FSZ:] = (di - hi.astype(F32)).astype(BF16)

    def precondition(v):
        out = []
        for k in range(6):
            y = mm(parts(v[:, face(k)]), dinv[k])
            y = y[:NR] + y[NR:]
            out.append(y[:, :FSZ] + y[:, FSZ:])
        return jnp.concatenate(out, axis=1)

    def apply_s(v):
        u = mm(parts(v), btm[...])
        u = u[:NR] + u[NR:]
        t = mm_t(parts(u), cmat[...])
        return (t[:NR] + t[NR:]) * alive

    m0 = [sum(eq(n0[k], f) for k in range(6)) * al[0] for f in range(NF + 2)]
    m1 = [sum(eq(n1[k], f) for k in range(6)) * al[1] for f in range(NF + 2)]
    mine_w = [jnp.where(e == 0, al[0], al[1] * (1.0 - m0[f])) for f in range(NF + 2)]
    their_w = [jnp.where(e == 1, al[0], al[1] * (1.0 - m0[f])) for f in range(NF + 2)]

    def hand_on(v, w):
        vbuf[v] = w
        out = [
            remote(
                vbuf.at[v, pl.ds(pl.multiple_of(8 * oe, 8), 8), :], vpar.at[v], vsend.at[v, 0],
                vrecv.at[v, 0], d, partner,
            )
        ]
        for side, name in enumerate((NF + 1, NF)):
            acc = jnp.zeros((NR, FSZ), F32)
            for k in range(6):
                acc += (eq(mine[k], name) * mine_w[name]) * w[:, face(k)]
            vnb[side, v] = acc
            for q in range(2):
                out.append(
                    remote(
                        vnb.at[side, v, 8 * q : 8 * q + 8, :], vnbr.at[side, e, v],
                        vsend.at[v, 1 + 2 * side + q], vrecv.at[v, 1 + 2 * side + e],
                        (nxt, prv)[side], 2 * h + q,
                    )
                )
        for c in out:
            c.start()
        return out

    w = precondition(assemble(0, rloc, rcp))
    vcp = []
    for i in range(3):
        t = apply_s(w)
        cps = send_all(1 + i, t)
        vcp += hand_on(i, w)
        if i < 2:
            w = precondition(assemble(1 + i, t, cps)) - w

    def fold(v):
        acc = v[:, face(0)]
        for k in range(1, 6):
            acc += v[:, face(k)]
        return acc

    prods = []
    for i in range(3):
        wi = vbuf[i]
        for j in range(3):
            prods.append(fold(wi * tvec[1 + j]))
        prods.append(fold(wi * tvec[0]))
    pads = [jnp.zeros((NR, FSZ), F32)] * 4
    for c in range(2):
        stack = jnp.concatenate((prods + pads)[8 * c : 8 * c + 8], axis=0)
        pay[0, c : c + 1, :] = jnp.sum(jnp.transpose(stack), axis=0, keepdims=True)
    ra[me_a] = pay[0]

    def plane_send(o):
        dd, xx, s = plane_peer(o)
        return remote(pay.at[0], ra.at[me_a], asend.at[s], arecv.at[me_a], dd, xx)

    def plane_from(o):
        _dd, _xx, s = plane_peer(o)
        return remote(pay.at[0], ra.at[s], asend.at[s], arecv.at[s], d, partner)

    def axis_send(o):
        dd, xx, s = axis_peer(o)
        return remote(pay.at[1], rb.at[zz], bsend.at[s], brecv.at[zz], dd, xx)

    def axis_from(o):
        _dd, _xx, s = axis_peer(o)
        return remote(pay.at[1], rb.at[s], bsend.at[s], brecv.at[s], d, partner)

    @pl.loop(1, 2 * npl)
    def _(o):
        plane_send(o).start()

    @pl.loop(1, 2 * npl)
    def _(o):
        plane_from(o).wait_recv()

    tot = ra[0]
    for s in range(1, 2 * npl):
        tot = tot + ra[s]
    pay[1] = tot
    rb[zz] = tot

    @pl.loop(1, nz)
    def _(o):
        axis_send(o).start()

    settle(3, cps)
    for c in vcp:
        c.wait_send()
    for v in range(3):
        remote(vpar.at[v], vpar.at[v], vsend.at[0, 0], vrecv.at[v, 0], d, partner).wait_recv()
        for side in range(2):
            for q in range(2):
                remote(
                    vnb.at[side, v, 0:8, :], vnbr.at[side, q, v], vsend.at[0, 0],
                    vrecv.at[v, 1 + 2 * side + q], d, partner,
                ).wait_recv()
    rows = pl.ds(pl.multiple_of(8 * e, 8), 8)
    for f in range(NF):
        free = 1.0 - jnp.maximum(m0[f], m1[f])
        wp = free * eq(lo_slot, f) * has_prev
        wn = free * eq(up_slot, f) * has_next
        for v in range(3):
            acc = wp * (vnbr[0, 0, v] + vnbr[0, 1, v]) + wn * (vnbr[1, 0, v] + vnbr[1, 1, v])
            for k in range(6):
                acc += (eq(mine[k], f) * mine_w[f]) * vbuf[v, rows, face(k)]
                acc += (eq(theirs[k], f) * their_w[f]) * vpar[v, :, face(k)]
            outb[v, f] = acc
        tp = eq(lo_slot, f) * has_prev
        tn = eq(up_slot, f) * has_next
        for ex in range(4):
            acc = tp * (rnb[ex, 0, 0, 1, rows, :] + rnb[ex, 0, 1, 1, rows, :])
            acc += tn * (rnb[ex, 1, 0, 1, rows, :] + rnb[ex, 1, 1, 1, rows, :])
            for k in range(6):
                acc += eq(mine[k], f) * tvec[ex, rows, face(k)]
                acc += eq(theirs[k], f) * rvec[ex, rows, face(k)]
            outb[3 + ex, f] = acc

    @pl.loop(1, 2 * npl)
    def _(o):
        plane_send(o).wait_send()

    @pl.loop(1, nz)
    def _(o):
        axis_from(o).wait_recv()

    @pl.loop(1, nz)
    def _(o):
        axis_send(o).wait_send()

    for c in shards:
        c.wait_send()
    tot = rb[0]
    for s in range(1, nz):
        tot = tot + rb[s]

    def pick(q):
        r = jnp.broadcast_to(tot[q // 8 : q // 8 + 1, :], (8, FSZ))
        at = (q % 8) * NR + 8 * e
        return jnp.sum(jnp.where(lane8 == sub8 + at, r, 0.0), axis=1, keepdims=True)

    g = [[pick(4 * i + j) for j in range(3)] for i in range(3)]
    gr = [pick(4 * i + 3) for i in range(3)]

    zero = jnp.zeros((8, 1), F32)
    pi = [zero + 1.0, zero, zero]
    rho = [zero, zero, zero]
    xc = [zero, zero, zero]
    rz = gr[0]
    for it in range(3):
        psp = zero
        for i in range(it + 1):
            for j in range(it + 1):
                psp += pi[i] * pi[j] * g[i][j]
        alpha = rz / psp
        xc = [xc[i] + alpha * pi[i] for i in range(3)]
        rho = [rho[i] - alpha * pi[i] for i in range(3)]
        if it == 2:
            break
        zc = [1.0 + rho[0], rho[0] + rho[1], rho[1] + rho[2]]
        new = zero
        for i in range(it + 2):
            s = gr[i]
            for j in range(it + 1):
                s += rho[j] * g[i][j]
            new += zc[i] * s
        beta = new / rz
        pi = [zc[i] + beta * pi[i] for i in range(3)]
        rz = new
    xb = [jnp.broadcast_to(c, (8, FSZ)) for c in xc]
    rbc = [jnp.broadcast_to(c, (8, FSZ)) for c in rho]
    for f in range(NF):
        sol[f] = xb[0] * outb[0, f] + xb[1] * outb[1, f] + xb[2] * outb[2, f]
        res[f] = outb[3, f] + rbc[0] * outb[4, f] + rbc[1] * outb[5, f] + rbc[2] * outb[6, f]


def per_device(nd, npl, elem_count, face_count, bound_slot, elem_face, density, coupling, ainv, loads):
    columns = jnp.swapaxes(coupling, 1, 2)
    smem = pl.BlockSpec(memory_space=pltpu.SMEM)
    vmem = pl.BlockSpec(memory_space=pltpu.VMEM)
    hbm = pl.BlockSpec(memory_space=pltpu.HBM)
    dma = pltpu.SemaphoreType.DMA
    nz = nd // npl
    out = pltpu.VMEM((NF, 8, FSZ), F32)
    vm = pltpu.VMEM
    return pl.pallas_call(
        functools.partial(kernel, nd, npl),
        out_shape=(out, out),
        in_specs=[smem, smem, smem, smem, hbm, hbm, hbm, hbm],
        out_specs=(vmem, vmem),
        scratch_shapes=[
            vm((TR, TR), BF16),
            vm((TR, TR), BF16),
            vm((TR, TR), BF16),
            vm((TR, TR), BF16),
            vm((2, TR), F32),
            vm((8, TR), BF16),
            vm((8, TR), BF16),
            vm((6, PK, FSZ), F32),
            vm((6, PK, FSZ), F32),
            vm((2, 2 * PK + 8, FSZ), F32),
            vm((2, 2, 2 * PK + 8, FSZ), F32),
            vm((8 * FSZ, FSZ), F32),
            vm((8 * BL, FSZ), F32),
            vm((8 * BL, FSZ), F32),
            vm((6, FSZ, 2 * FSZ), BF16),
            vm((4, NR, TR), F32),
            vm((4, 2, 2, NR, FSZ), F32),
            vm((4, NR, TR), F32),
            vm((4, 2, 2, 2, NR, FSZ), F32),
            vm((3, NR, TR), F32),
            vm((3, 8, TR), F32),
            vm((2, 3, NR, FSZ), F32),
            vm((2, 2, 3, 8, FSZ), F32),
            vm((7, NF, 8, FSZ), F32),
            vm((2, 2, FSZ), F32),
            vm((2 * npl, 2, FSZ), F32),
            vm((nz, 2, FSZ), F32),
            pltpu.SemaphoreType.REGULAR((2,)),
            dma((4,)), dma((3,)), dma((4,)), dma, dma, dma((6,)), dma((6,)),
            dma((4, 5)), dma((4, 5)), dma((3, 5)), dma((3, 5)),
            dma((2 * npl,)), dma((2 * npl,)), dma((nz,)), dma((nz,)),
        ],
        compiler_params=pltpu.CompilerParams(
            collective_id=0, has_side_effects=True, vmem_limit_bytes=VMEM_ALL
        ),
        name="condense_cg",
    )(elem_count, face_count, bound_slot, elem_face, density, columns, loads, ainv)


def solution(mesh):
    placed = (
        P("dom"),
        P("dom"),
        P("dom", None),
        P("dom", None),
        P("dom", None),
        P("dom", None, "rhs"),
        P(),
        P("dom", "rhs", None),
    )
    nd = mesh.shape["dom"]
    npl = min(PLANE, nd // 2)
    return jax.shard_map(
        functools.partial(per_device, nd, npl),
        mesh=mesh,
        in_specs=placed,
        out_specs=(P("dom", "rhs", None), P("dom", "rhs", None)),
        check_vma=False,
    )
```

```python
import functools

import jax
import jax.numpy as jnp
from jax import lax
from jax.experimental import pallas as pl
from jax.experimental.pallas import tpu as pltpu
from jax.sharding import PartitionSpec as P

FSZ = 128
NF = 9
TR = 768
NR = 16
PLANE = 8
VMEM_ALL = 62 * 1024 * 1024
PK = 72
BL = 16
F32 = jnp.float32
BF16 = jnp.bfloat16
MESH = pl.DeviceIdType.MESH


def parts(v):
    hi = v.astype(BF16).astype(F32)
    return jnp.concatenate([hi, v - hi], axis=0).astype(BF16)


def mm(a, b):
    return jnp.dot(a, b, preferred_element_type=F32)


def mm_t(a, b):
    return lax.dot_general(a, b, (((1,), (1,)), ((), ())), preferred_element_type=F32)


def face(k):
    return slice(k * FSZ, (k + 1) * FSZ)


def kernel(
    nd, npl,
    ec, fc, bs_in, ef_in, dens, coup, loads, ainv, sol, res,
    bs, ef, amt, craw, cmat, btm, den, lown, lrecv, dloc, dpar, dsnd, dnbr, msc, wrow, zrow, dinv,
    tvec, tnb, rvec, rnb, vbuf, vpar, vnb, vnbr, outb, pay, ra, rb,
    near, lsem, csend, crecv, lsend, lrecvs, dsend, drecv, tsend, trecv, vsend, vrecv,
    asend, arecv, bsend, brecv,
):
    d = lax.axis_index("dom")
    x = lax.axis_index("rhs")
    e = lax.rem(x, 2)
    h = x // 2
    oe = 1 - e
    partner = 2 * h + oe
    nxt, prv = lax.rem(d + 1, nd), lax.rem(d + nd - 1, nd)
    nz = nd // npl
    zz, jj = d // npl, lax.rem(d, npl)
    me_a = jj * 2 + e

    def dev(dd, xx):
        return {"dom": dd, "rhs": xx}

    def rows_of(s):
        return craw.at[pl.ds(pl.multiple_of(192 * s, 64), 192)]

    loc = [
        pltpu.make_async_copy(dens, den, lsem.at[0]),
        pltpu.make_async_copy(coup.at[e], rows_of(x), lsem.at[1]),
        pltpu.make_async_copy(loads.at[e], lown, lsem.at[2]),
        pltpu.make_async_copy(ainv, amt, lsem.at[3]),
        pltpu.make_async_copy(bs_in, bs, lsem.at[4]),
        pltpu.make_async_copy(ef_in, ef, lsem.at[5]),
    ]

    bar = pltpu.get_barrier_semaphore()

    def hello(dd, xx):
        pl.semaphore_signal(bar, inc=1, device_id=dev(dd, xx), device_id_type=MESH)

    for o in range(1, 4):
        hello(d, lax.rem(x + o, 4))
    for q in range(2):
        hello(nxt, 2 * h + q)
        hello(prv, 2 * h + q)
    beside = lax.rem(partner + 2, 4)
    hello(nxt, beside)
    hello(prv, beside)

    def plane_peer(o):
        s = lax.rem(me_a + o, 2 * npl)
        return zz * npl + s // 2, 2 * h + lax.rem(s, 2), s

    def axis_peer(o):
        s = lax.rem(zz + o, nz)
        return s * npl + jj, x, s

    @pl.loop(1, 2 * npl)
    def _(o):
        dd, xx, _s = plane_peer(o)
        hello(dd, xx)

    above, below = lax.rem(zz + 1, nz) * npl + jj, lax.rem(zz + nz - 1, nz) * npl + jj
    hello(above, x)
    hello(below, x)

    for c in loc:
        c.start()
    pl.semaphore_wait(bar, 3 + 6 + 2 * npl - 1 + 2)

    def remote(src, dst, ssem, rsem, dd, xx):
        return pltpu.make_async_remote_copy(
            src_ref=src, dst_ref=dst, send_sem=ssem, recv_sem=rsem,
            device_id=dev(dd, xx), device_id_type=MESH,
        )

    far = lax.rem(x + 2, 4)
    shards = [
        remote(coup.at[oe], rows_of(x), csend.at[0], crecv.at[x], d, partner),
        remote(coup.at[e], rows_of(x), csend.at[2], crecv.at[x], d, far),
        remote(coup.at[oe], rows_of(x), csend.at[1], crecv.at[x], d, beside),
    ]

    def shard_from(s):
        return remote(coup.at[0], rows_of(s), csend.at[0], crecv.at[s], d, partner)

    for c in shards:
        c.start()
    lcopy = remote(loads.at[oe], lrecv, lsend, lrecvs, d, partner)
    lcopy.start()

    for _r in range(nz // 2 - 1):
        pl.semaphore_signal(near.at[0], inc=1, device_id=dev(above, x), device_id_type=MESH)
        pl.semaphore_signal(near.at[1], inc=1, device_id=dev(below, x), device_id_type=MESH)
        pl.semaphore_wait(near.at[0], 1)
        pl.semaphore_wait(near.at[1], 1)

    loc[0].wait()
    scal = lax.rsqrt(den[pl.ds(e, 1), :])

    for c in loc[4:]:
        c.wait()
    alive = (e < ec[0]).astype(F32)
    al = [(q < ec[0]).astype(F32) for q in range(2)]
    n0 = [ef[0, k] for k in range(6)]
    n1 = [ef[1, k] for k in range(6)]
    mine = [ef[e, k] for k in range(6)]
    theirs = [ef[oe, k] for k in range(6)]
    lo_slot, up_slot = bs[0, 0], bs[0, 1]
    has_prev = (d > 0).astype(F32)
    has_next = (d < nd - 1).astype(F32)

    def eq(a, b):
        return (a == b).astype(F32)

    to_next = [[eq(mine[k], up_slot) for k in range(6)], [eq(mine[k], NF + 1) for k in range(6)]]
    to_prev = [[eq(mine[k], lo_slot) for k in range(6)], [eq(mine[k], NF) for k in range(6)]]
    same = [[eq(mine[k], theirs[q]) for q in range(6)] for k in range(6)]
    from_prev = [
        [eq(mine[k], NF) * has_prev, eq(mine[k], lo_slot) * has_prev] for k in range(6)
    ]
    from_next = [
        [eq(mine[k], NF + 1) * has_next, eq(mine[k], up_slot) * has_next] for k in range(6)
    ]

    row64 = lax.broadcasted_iota(jnp.int32, (64, FSZ), 0)
    lane64 = lax.broadcasted_iota(jnp.int32, (64, FSZ), 1)
    loc[1].wait()
    loc[3].wait()
    amat = amt[...]
    for t in range(2):
        p = lax.rem(h + t, 2)
        if t == 0:
            shard_from(partner).wait_recv()
        else:
            shard_from(2 * p).wait_recv()
            shard_from(2 * p + 1).wait_recv()
        at = pl.multiple_of(p * 384, 128)
        for k in range(3):
            rows = pl.ds(at + k * FSZ, FSZ)
            ck = (craw[rows, :].astype(F32) * scal).astype(BF16)
            cmat[rows, :] = ck
            bt = mm(ck, amat).astype(BF16)
            btm[rows, :] = bt
            dk = mm_t(bt, ck) * (0.5 * alive)
            dk = dk + jnp.transpose(dk)
            lower = pltpu.roll(dk[64:, :], 64, 1)
            dloc[3 * p + k, 0:64, :] = jnp.where((lane64 < 64) & (lane64 < row64), lower, dk[:64, :])
            tail = jnp.sum(jnp.where(lane64 == row64 + 64, dk[64:, :], 0.0), axis=0, keepdims=True)
            dloc[3 * p + k, 64:, :] = jnp.broadcast_to(tail, (8, FSZ))

    xl, xr = lax.rem(x + 3, 4), lax.rem(x + 1, 4)
    dcp = [
        remote(dloc.at[0:3], dpar.at[0:3], dsend.at[0], drecv.at[0], d, xl),
        remote(dloc.at[3:6], dpar.at[3:6], dsend.at[1], drecv.at[1], d, xr),
    ]
    for side, table in enumerate((to_next, to_prev)):
        for s in range(2):
            acc = table[s][0] * dloc[0]
            for k in range(1, 6):
                acc += table[s][k] * dloc[k]
            dsnd[side, s * PK : (s + 1) * PK, :] = acc
        slot = up_slot if side == 0 else lo_slot
        live = (slot < fc[0]).astype(F32)
        dsnd[side, 2 * PK :, :] = jnp.full((8, FSZ), 1.0, F32) * live
    for side, dd in enumerate((nxt, prv)):
        for q, xx in enumerate((x, (partner, beside)[side])):
            c = remote(
                dsnd.at[side], dnbr.at[side, e], dsend.at[2 + 2 * side + q],
                drecv.at[2 + 2 * side + e], dd, xx,
            )
            dcp.append(c)

    for c in dcp[2:] + dcp[:2]:
        c.start()

    def send_all(ex, t):
        tvec[ex] = t
        out = [remote(tvec.at[ex], rvec.at[ex], tsend.at[ex, 0], trecv.at[ex, 0], d, partner)]
        for side, table in enumerate((to_next, to_prev)):
            for s in range(2):
                acc = table[s][0] * t[:, face(0)]
                for k in range(1, 6):
                    acc += table[s][k] * t[:, face(k)]
                tnb[ex, side, s] = acc
            dd = (nxt, prv)[side]
            for q in range(2):
                c = remote(
                    tnb.at[ex, side], rnb.at[ex, side, e], tsend.at[ex, 1 + 2 * side + q],
                    trecv.at[ex, 1 + 2 * side + e], dd, 2 * h + q,
                )
                c.start()
                out.append(c)
        out[0].start()
        return out

    def settle(ex, cps):
        for c in cps:
            c.wait_send()
        remote(tvec.at[ex], rvec.at[ex], tsend.at[ex, 0], trecv.at[ex, 0], d, partner).wait_recv()
        for side in range(2):
            for q in range(2):
                remote(
                    tnb.at[ex, side], rnb.at[ex, side, q], tsend.at[ex, 0],
                    trecv.at[ex, 1 + 2 * side + q], d, partner,
                ).wait_recv()

    def assemble(ex, t, cps):
        settle(ex, cps)
        pv = [rnb[ex, 0, 0, s] + rnb[ex, 0, 1, s] for s in range(2)]
        nv = [rnb[ex, 1, 0, s] + rnb[ex, 1, 1, s] for s in range(2)]
        other = [rvec[ex, :, face(q)] for q in range(6)]
        cols = []
        for k in range(6):
            acc = t[:, face(k)]
            for q in range(6):
                acc += same[k][q] * other[q]
            acc += from_prev[k][0] * pv[0] + from_prev[k][1] * pv[1]
            acc += from_next[k][0] * nv[0] + from_next[k][1] * nv[1]
            cols.append(acc)
        return jnp.concatenate(cols, axis=1)

    lcopy.wait()
    loc[2].wait()
    srow = scal
    wgt = [
        (lown[...].astype(F32) * srow).astype(BF16).astype(F32),
        (lrecv[...].astype(F32) * srow).astype(BF16).astype(F32),
    ]
    low = e == 0
    weighted = jnp.concatenate(
        [jnp.where(low, wgt[0], wgt[1]), jnp.where(low, wgt[1], wgt[0])], axis=0
    ).astype(BF16)
    forced = mm(weighted, amat).astype(BF16)
    rloc = mm_t(forced, cmat[...]) * alive
    rcp = send_all(0, rloc)

    for c in dcp:
        c.wait_send()
    remote(dloc.at[0:3], dpar.at[0:3], dsend.at[0], drecv.at[0], d, partner).wait_recv()
    remote(dloc.at[3:6], dpar.at[3:6], dsend.at[0], drecv.at[1], d, partner).wait_recv()
    for side in range(2):
        for q in range(2):
            remote(
                dsnd.at[side], dnbr.at[side, q], dsend.at[0], drecv.at[2 + 2 * side + q], d, partner
            ).wait_recv()
    row = lax.broadcasted_iota(jnp.int32, (FSZ, FSZ), 0)
    col = lax.broadcasted_iota(jnp.int32, (FSZ, FSZ), 1)
    eye = (row == col).astype(F32)
    srows, scols = [], []
    for k in range(6):
        acc = dloc[k]
        for q in range(6):
            acc += same[k][q] * dpar[q]
        for s in range(2):
            at = slice(s * PK, (s + 1) * PK)
            acc += from_prev[k][s] * (dnbr[0, 0, at, :] + dnbr[0, 1, at, :])
            acc += from_next[k][s] * (dnbr[1, 0, at, :] + dnbr[1, 1, at, :])
        flag = jnp.full((1, FSZ), 1.0, F32) * (mine[k] < fc[0]).astype(F32)
        flag = jnp.where(mine[k] == NF, dnbr[0, 0, 2 * PK : 2 * PK + 1, :], flag)
        flag = jnp.where(mine[k] == NF + 1, dnbr[1, 0, 2 * PK : 2 * PK + 1, :], flag)
        body, tail = acc[:64, :], acc[64:65, :]
        keep = jnp.where(lane64 == row64, 0.5, 1.0)
        up = jnp.where(lane64 >= row64, body * keep, 0.0)
        dn = pltpu.roll(jnp.where(lane64 < row64, body, 0.0), 64, 1)
        dn = dn + jnp.where(lane64 == row64 + 64, 0.5 * tail, 0.0)
        half = jnp.concatenate([up, dn], axis=0)
        acc = half + jnp.transpose(half)
        acc = jnp.where(flag * alive > 0.5, acc, eye)
        diag = acc * eye
        srow_k = lax.rsqrt(jnp.sum(diag, axis=0, keepdims=True))
        scol_k = lax.rsqrt(jnp.sum(diag, axis=1, keepdims=True))
        srows.append(srow_k)
        scols.append(scol_k)
        msc[k * FSZ : (k + 1) * FSZ, :] = acc * srow_k * scol_k

    msc[6 * FSZ : 7 * FSZ, :] = eye
    msc[7 * FSZ :, :] = eye
    sub8 = lax.broadcasted_iota(jnp.int32, (8, FSZ), 0)
    lane8 = lax.broadcasted_iota(jnp.int32, (8, FSZ), 1)
    laneb = lax.broadcasted_iota(jnp.int32, (BL, FSZ), 1)
    rowb = lax.broadcasted_iota(jnp.int32, (BL, FSZ), 0)

    def at_lane(r, i):
        return jnp.broadcast_to(r[:, i : i + 1], (8, FSZ))

    def invert8(p):
        p = dict(p)

        def key(a, b):
            return (a, b) if a <= b else (b, a)

        for i in range(8):
            dinv_i = 1.0 / p[i, i]
            old = {a: p[key(a, i)] for a in range(8) if a != i}
            fac = {a: old[a] * dinv_i for a in old}
            for a in old:
                for b in old:
                    if a <= b:
                        p[a, b] = p[a, b] - fac[a] * old[b]
            for a in old:
                p[key(a, i)] = fac[a]
            p[i, i] = -dinv_i
        return {(a, b): p[key(a, b)] for a in range(8) for b in range(8)}

    for base in range(0, FSZ, BL):
        r = [msc[pl.ds(base + i, 8, stride=FSZ), :] for i in range(BL)]
        for lo in range(0, BL, 8):
            at = base + lo
            neg = invert8({
                (a, b): at_lane(r[lo + a], at + b) for a in range(8) for b in range(a, 8)
            })
            inside = (lane8 >= at) & (lane8 < at + 8)
            unit = [(lane8 == at + a).astype(F32) for a in range(8)]
            plain = [jnp.where(inside, -unit[b], r[lo + b]) for b in range(8)]
            y = []
            for a in range(8):
                acc = neg[a, 0] * plain[0]
                for b in range(1, 8):
                    acc += neg[a, b] * plain[b]
                y.append(acc)
            for i in range(lo + 8, BL):
                acc = jnp.where(inside, 0.0, r[i])
                for a in range(8):
                    acc += at_lane(r[i], at + a) * y[a]
                r[i] = acc
            for a in range(8):
                i = lo + a
                wrow[8 * i : 8 * i + 8, :] = r[i] - unit[a]
                zrow[8 * i : 8 * i + 8, :] = jnp.where(inside, unit[a], 0.0) - y[a]
        two = jnp.where(laneb == rowb + base, 2.0, 0.0)
        for k in range(6):
            xm = wrow[pl.ds(k, BL, stride=8), :]
            ym = zrow[pl.ds(k, BL, stride=8), :]
            x1 = xm.astype(BF16)
            x2 = (xm - x1.astype(F32)).astype(BF16)
            y1 = ym.astype(BF16)
            y2 = (ym - y1.astype(F32)).astype(BF16)
            xs = jnp.concatenate([x1, x1, x2], axis=0)
            ys = jnp.concatenate([y1, y2, y1], axis=0)
            upd = lax.dot_general(xs, ys, (((0,), (0,)), ((), ())), preferred_element_type=F32)
            mat = slice(k * FSZ, (k + 1) * FSZ)
            msc[mat, :] = msc[mat, :] - upd
            own_rows = slice(k * FSZ + base, k * FSZ + base + BL)
            msc[own_rows, :] = msc[own_rows, :] - two

    for k in range(6):
        di = -(msc[k * FSZ : (k + 1) * FSZ, :] * srows[k] * scols[k])
        hi = di.astype(BF16)
        dinv[k, :, 0:FSZ] = hi
        dinv[k, :, FSZ:] = (di - hi.astype(F32)).astype(BF16)

    def precondition(v):
        out = []
        for k in range(6):
            y = mm(parts(v[:, face(k)]), dinv[k])
            y = y[:NR] + y[NR:]
            out.append(y[:, :FSZ] + y[:, FSZ:])
        return jnp.concatenate(out, axis=1)

    def apply_s(v):
        u = mm(parts(v), btm[...])
        u = u[:NR] + u[NR:]
        t = mm_t(parts(u), cmat[...])
        return (t[:NR] + t[NR:]) * alive

    m0 = [sum(eq(n0[k], f) for k in range(6)) * al[0] for f in range(NF + 2)]
    m1 = [sum(eq(n1[k], f) for k in range(6)) * al[1] for f in range(NF + 2)]
    mine_w = [jnp.where(e == 0, al[0], al[1] * (1.0 - m0[f])) for f in range(NF + 2)]
    their_w = [jnp.where(e == 1, al[0], al[1] * (1.0 - m0[f])) for f in range(NF + 2)]

    def hand_on(v, w):
        vbuf[v] = w
        out = [
            remote(
                vbuf.at[v, pl.ds(pl.multiple_of(8 * oe, 8), 8), :], vpar.at[v], vsend.at[v, 0],
                vrecv.at[v, 0], d, partner,
            )
        ]
        for side, name in enumerate((NF + 1, NF)):
            acc = jnp.zeros((NR, FSZ), F32)
            for k in range(6):
                acc += (eq(mine[k], name) * mine_w[name]) * w[:, face(k)]
            vnb[side, v] = acc
            for q in range(2):
                out.append(
                    remote(
                        vnb.at[side, v, 8 * q : 8 * q + 8, :], vnbr.at[side, e, v],
                        vsend.at[v, 1 + 2 * side + q], vrecv.at[v, 1 + 2 * side + e],
                        (nxt, prv)[side], 2 * h + q,
                    )
                )
        for c in out:
            c.start()
        return out

    w = precondition(assemble(0, rloc, rcp))
    vcp = []
    for i in range(3):
        vcp += hand_on(i, w)
        t = apply_s(w)
        cps = send_all(1 + i, t)
        if i < 2:
            w = precondition(assemble(1 + i, t, cps)) - w

    def fold(v):
        acc = v[:, face(0)]
        for k in range(1, 6):
            acc += v[:, face(k)]
        return acc

    prods = []
    for i in range(3):
        wi = vbuf[i]
        for j in range(3):
            prods.append(fold(wi * tvec[1 + j]))
        prods.append(fold(wi * tvec[0]))
    pads = [jnp.zeros((NR, FSZ), F32)] * 4
    for c in range(2):
        stack = jnp.concatenate((prods + pads)[8 * c : 8 * c + 8], axis=0)
        pay[0, c : c + 1, :] = jnp.sum(jnp.transpose(stack), axis=0, keepdims=True)
    ra[me_a] = pay[0]

    def plane_send(o):
        dd, xx, s = plane_peer(o)
        return remote(pay.at[0], ra.at[me_a], asend.at[s], arecv.at[me_a], dd, xx)

    def plane_from(o):
        _dd, _xx, s = plane_peer(o)
        return remote(pay.at[0], ra.at[s], asend.at[s], arecv.at[s], d, partner)

    def axis_send(o):
        dd, xx, s = axis_peer(o)
        return remote(pay.at[1], rb.at[zz], bsend.at[s], brecv.at[zz], dd, xx)

    def axis_from(o):
        _dd, _xx, s = axis_peer(o)
        return remote(pay.at[1], rb.at[s], bsend.at[s], brecv.at[s], d, partner)

    @pl.loop(1, 2 * npl)
    def _(o):
        plane_send(o).start()

    @pl.loop(1, 2 * npl)
    def _(o):
        plane_from(o).wait_recv()

    tot = ra[0]
    for s in range(1, 2 * npl):
        tot = tot + ra[s]
    pay[1] = tot
    rb[zz] = tot

    @pl.loop(1, nz)
    def _(o):
        axis_send(o).start()

    settle(3, cps)
    for c in vcp:
        c.wait_send()
    for v in range(3):
        remote(vpar.at[v], vpar.at[v], vsend.at[0, 0], vrecv.at[v, 0], d, partner).wait_recv()
        for side in range(2):
            for q in range(2):
                remote(
                    vnb.at[side, v, 0:8, :], vnbr.at[side, q, v], vsend.at[0, 0],
                    vrecv.at[v, 1 + 2 * side + q], d, partner,
                ).wait_recv()
    rows = pl.ds(pl.multiple_of(8 * e, 8), 8)
    for f in range(NF):
        free = 1.0 - jnp.maximum(m0[f], m1[f])
        wp = free * eq(lo_slot, f) * has_prev
        wn = free * eq(up_slot, f) * has_next
        for v in range(3):
            acc = wp * (vnbr[0, 0, v] + vnbr[0, 1, v]) + wn * (vnbr[1, 0, v] + vnbr[1, 1, v])
            for k in range(6):
                acc += (eq(mine[k], f) * mine_w[f]) * vbuf[v, rows, face(k)]
                acc += (eq(theirs[k], f) * their_w[f]) * vpar[v, :, face(k)]
            outb[v, f] = acc
        tp = eq(lo_slot, f) * has_prev
        tn = eq(up_slot, f) * has_next
        for ex in range(4):
            acc = tp * (rnb[ex, 0, 0, 1, rows, :] + rnb[ex, 0, 1, 1, rows, :])
            acc += tn * (rnb[ex, 1, 0, 1, rows, :] + rnb[ex, 1, 1, 1, rows, :])
            for k in range(6):
                acc += eq(mine[k], f) * tvec[ex, rows, face(k)]
                acc += eq(theirs[k], f) * rvec[ex, rows, face(k)]
            outb[3 + ex, f] = acc

    @pl.loop(1, 2 * npl)
    def _(o):
        plane_send(o).wait_send()

    @pl.loop(1, nz)
    def _(o):
        axis_from(o).wait_recv()

    @pl.loop(1, nz)
    def _(o):
        axis_send(o).wait_send()

    for c in shards:
        c.wait_send()
    tot = rb[0]
    for s in range(1, nz):
        tot = tot + rb[s]

    def pick(q):
        r = jnp.broadcast_to(tot[q // 8 : q // 8 + 1, :], (8, FSZ))
        at = (q % 8) * NR + 8 * e
        return jnp.sum(jnp.where(lane8 == sub8 + at, r, 0.0), axis=1, keepdims=True)

    g = [[pick(4 * i + j) for j in range(3)] for i in range(3)]
    gr = [pick(4 * i + 3) for i in range(3)]

    zero = jnp.zeros((8, 1), F32)
    pi = [zero + 1.0, zero, zero]
    rho = [zero, zero, zero]
    xc = [zero, zero, zero]
    rz = gr[0]
    for it in range(3):
        psp = zero
        for i in range(it + 1):
            for j in range(it + 1):
                psp += pi[i] * pi[j] * g[i][j]
        alpha = rz / psp
        xc = [xc[i] + alpha * pi[i] for i in range(3)]
        rho = [rho[i] - alpha * pi[i] for i in range(3)]
        if it == 2:
            break
        zc = [1.0 + rho[0], rho[0] + rho[1], rho[1] + rho[2]]
        new = zero
        for i in range(it + 2):
            s = gr[i]
            for j in range(it + 1):
                s += rho[j] * g[i][j]
            new += zc[i] * s
        beta = new / rz
        pi = [zc[i] + beta * pi[i] for i in range(3)]
        rz = new
    xb = [jnp.broadcast_to(c, (8, FSZ)) for c in xc]
    rbc = [jnp.broadcast_to(c, (8, FSZ)) for c in rho]
    for f in range(NF):
        sol[f] = xb[0] * outb[0, f] + xb[1] * outb[1, f] + xb[2] * outb[2, f]
        res[f] = outb[3, f] + rbc[0] * outb[4, f] + rbc[1] * outb[5, f] + rbc[2] * outb[6, f]


def per_device(nd, npl, elem_count, face_count, bound_slot, elem_face, density, coupling, ainv, loads):
    columns = jnp.swapaxes(coupling, 1, 2)
    smem = pl.BlockSpec(memory_space=pltpu.SMEM)
    vmem = pl.BlockSpec(memory_space=pltpu.VMEM)
    hbm = pl.BlockSpec(memory_space=pltpu.HBM)
    dma = pltpu.SemaphoreType.DMA
    nz = nd // npl
    out = pltpu.VMEM((NF, 8, FSZ), F32)
    vm = pltpu.VMEM
    return pl.pallas_call(
        functools.partial(kernel, nd, npl),
        out_shape=(out, out),
        in_specs=[smem, smem] + [hbm] * 6,
        out_specs=(vmem, vmem),
        scratch_shapes=[
            pltpu.SMEM((1, 2), jnp.int32),
            pltpu.SMEM((2, 6), jnp.int32),
            vm((TR, TR), BF16),
            vm((TR, TR), BF16),
            vm((TR, TR), BF16),
            vm((TR, TR), BF16),
            vm((2, TR), F32),
            vm((8, TR), BF16),
            vm((8, TR), BF16),
            vm((6, PK, FSZ), F32),
            vm((6, PK, FSZ), F32),
            vm((2, 2 * PK + 8, FSZ), F32),
            vm((2, 2, 2 * PK + 8, FSZ), F32),
            vm((8 * FSZ, FSZ), F32),
            vm((8 * BL, FSZ), F32),
            vm((8 * BL, FSZ), F32),
            vm((6, FSZ, 2 * FSZ), BF16),
            vm((4, NR, TR), F32),
            vm((4, 2, 2, NR, FSZ), F32),
            vm((4, NR, TR), F32),
            vm((4, 2, 2, 2, NR, FSZ), F32),
            vm((3, NR, TR), F32),
            vm((3, 8, TR), F32),
            vm((2, 3, NR, FSZ), F32),
            vm((2, 2, 3, 8, FSZ), F32),
            vm((7, NF, 8, FSZ), F32),
            vm((2, 2, FSZ), F32),
            vm((2 * npl, 2, FSZ), F32),
            vm((nz, 2, FSZ), F32),
            pltpu.SemaphoreType.REGULAR((2,)),
            dma((6,)), dma((3,)), dma((4,)), dma, dma, dma((6,)), dma((6,)),
            dma((4, 5)), dma((4, 5)), dma((3, 5)), dma((3, 5)),
            dma((2 * npl,)), dma((2 * npl,)), dma((nz,)), dma((nz,)),
        ],
        compiler_params=pltpu.CompilerParams(
            collective_id=0, has_side_effects=True, vmem_limit_bytes=VMEM_ALL
        ),
        name="condense_cg",
    )(elem_count, face_count, bound_slot, elem_face, density, columns, loads, ainv)


def solution(mesh):
    placed = (
        P("dom"),
        P("dom"),
        P("dom", None),
        P("dom", None),
        P("dom", None),
        P("dom", None, "rhs"),
        P(),
        P("dom", "rhs", None),
    )
    nd = mesh.shape["dom"]
    npl = min(PLANE, nd // 2)
    return jax.shard_map(
        functools.partial(per_device, nd, npl),
        mesh=mesh,
        in_specs=placed,
        out_specs=(P("dom", "rhs", None), P("dom", "rhs", None)),
        check_vma=False,
    )
```

```python
import functools

import jax
import jax.numpy as jnp
from jax import lax
from jax.experimental import pallas as pl
from jax.experimental.pallas import tpu as pltpu
from jax.sharding import PartitionSpec as P

FSZ = 128
NF = 9
TR = 768
NR = 16
PLANE = 8
VMEM_ALL = 62 * 1024 * 1024
PK = 72
BL = 16
F32 = jnp.float32
BF16 = jnp.bfloat16
MESH = pl.DeviceIdType.MESH


def parts(v):
    hi = v.astype(BF16).astype(F32)
    return jnp.concatenate([hi, v - hi], axis=0).astype(BF16)


def mm(a, b):
    return jnp.dot(a, b, preferred_element_type=F32)


def mm_t(a, b):
    return lax.dot_general(a, b, (((1,), (1,)), ((), ())), preferred_element_type=F32)


def face(k):
    return slice(k * FSZ, (k + 1) * FSZ)


def kernel(
    nd, npl,
    ec, fc, bs_in, ef_in, dens, coup, loads, ainv, sol, res,
    bs, ef, amt, craw, cmat, btm, den, lown, lrecv, dloc, dpar, dsnd, dnbr, msc, wrow, zrow, dinv,
    tvec, tnb, rvec, rnb, vbuf, vpar, vnb, vnbr, outb, pay, ra, rb,
    near, lsem, csend, crecv, lsend, lrecvs, dsend, drecv, tsend, trecv, vsend, vrecv,
    asend, arecv, bsend, brecv,
):
    d = lax.axis_index("dom")
    x = lax.axis_index("rhs")
    e = lax.rem(x, 2)
    h = x // 2
    oe = 1 - e
    partner = 2 * h + oe
    nxt, prv = lax.rem(d + 1, nd), lax.rem(d + nd - 1, nd)
    nz = nd // npl
    zz, jj = d // npl, lax.rem(d, npl)
    me_a = jj * 2 + e

    def dev(dd, xx):
        return {"dom": dd, "rhs": xx}

    def rows_of(s):
        return craw.at[pl.ds(pl.multiple_of(192 * s, 64), 192)]

    loc = [
        pltpu.make_async_copy(dens, den, lsem.at[0]),
        pltpu.make_async_copy(coup.at[e], rows_of(x), lsem.at[1]),
        pltpu.make_async_copy(loads.at[e], lown, lsem.at[2]),
        pltpu.make_async_copy(ainv, amt, lsem.at[3]),
        pltpu.make_async_copy(bs_in, bs, lsem.at[4]),
        pltpu.make_async_copy(ef_in, ef, lsem.at[5]),
    ]

    bar = pltpu.get_barrier_semaphore()

    def hello(dd, xx):
        pl.semaphore_signal(bar, inc=1, device_id=dev(dd, xx), device_id_type=MESH)

    for o in range(1, 4):
        hello(d, lax.rem(x + o, 4))
    for q in range(2):
        hello(nxt, 2 * h + q)
        hello(prv, 2 * h + q)
    beside = lax.rem(partner + 2, 4)
    hello(nxt, beside)
    hello(prv, beside)

    def plane_peer(o):
        s = lax.rem(me_a + o, 2 * npl)
        return zz * npl + s // 2, 2 * h + lax.rem(s, 2), s

    def axis_peer(o):
        s = lax.rem(zz + o, nz)
        return s * npl + jj, x, s

    @pl.loop(1, 2 * npl)
    def _(o):
        dd, xx, _s = plane_peer(o)
        hello(dd, xx)

    above, below = lax.rem(zz + 1, nz) * npl + jj, lax.rem(zz + nz - 1, nz) * npl + jj
    hello(above, x)
    hello(below, x)

    for c in loc:
        c.start()
    pl.semaphore_wait(bar, 3 + 6 + 2 * npl - 1 + 2)

    def remote(src, dst, ssem, rsem, dd, xx):
        return pltpu.make_async_remote_copy(
            src_ref=src, dst_ref=dst, send_sem=ssem, recv_sem=rsem,
            device_id=dev(dd, xx), device_id_type=MESH,
        )

    far = lax.rem(x + 2, 4)
    shards = [
        remote(coup.at[oe], rows_of(x), csend.at[0], crecv.at[x], d, partner),
        remote(coup.at[e], rows_of(x), csend.at[2], crecv.at[x], d, far),
        remote(coup.at[oe], rows_of(x), csend.at[1], crecv.at[x], d, beside),
    ]

    def shard_from(s):
        return remote(coup.at[0], rows_of(s), csend.at[0], crecv.at[s], d, partner)

    for c in shards:
        c.start()
    lcopy = remote(loads.at[oe], lrecv, lsend, lrecvs, d, partner)
    lcopy.start()

    for _r in range(nz // 2 - 1):
        pl.semaphore_signal(near.at[0], inc=1, device_id=dev(above, x), device_id_type=MESH)
        pl.semaphore_signal(near.at[1], inc=1, device_id=dev(below, x), device_id_type=MESH)
        pl.semaphore_wait(near.at[0], 1)
        pl.semaphore_wait(near.at[1], 1)

    loc[0].wait()
    scal = lax.rsqrt(den[pl.ds(e, 1), :])

    for c in loc[4:]:
        c.wait()
    alive = (e < ec[0]).astype(F32)
    al = [(q < ec[0]).astype(F32) for q in range(2)]
    n0 = [ef[0, k] for k in range(6)]
    n1 = [ef[1, k] for k in range(6)]
    mine = [ef[e, k] for k in range(6)]
    theirs = [ef[oe, k] for k in range(6)]
    lo_slot, up_slot = bs[0, 0], bs[0, 1]
    has_prev = (d > 0).astype(F32)
    has_next = (d < nd - 1).astype(F32)

    def eq(a, b):
        return (a == b).astype(F32)

    to_next = [[eq(mine[k], up_slot) for k in range(6)], [eq(mine[k], NF + 1) for k in range(6)]]
    to_prev = [[eq(mine[k], lo_slot) for k in range(6)], [eq(mine[k], NF) for k in range(6)]]
    same = [[eq(mine[k], theirs[q]) for q in range(6)] for k in range(6)]
    from_prev = [
        [eq(mine[k], NF) * has_prev, eq(mine[k], lo_slot) * has_prev] for k in range(6)
    ]
    from_next = [
        [eq(mine[k], NF + 1) * has_next, eq(mine[k], up_slot) * has_next] for k in range(6)
    ]

    row64 = lax.broadcasted_iota(jnp.int32, (64, FSZ), 0)
    lane64 = lax.broadcasted_iota(jnp.int32, (64, FSZ), 1)
    loc[1].wait()
    loc[3].wait()
    amat = amt[...]
    for t in range(2):
        p = lax.rem(h + t, 2)
        if t == 0:
            shard_from(partner).wait_recv()
        else:
            shard_from(2 * p).wait_recv()
            shard_from(2 * p + 1).wait_recv()
        at = pl.multiple_of(p * 384, 128)
        for k in range(3):
            rows = pl.ds(at + k * FSZ, FSZ)
            ck = (craw[rows, :].astype(F32) * scal).astype(BF16)
            cmat[rows, :] = ck
            bt = mm(ck, amat).astype(BF16)
            btm[rows, :] = bt
            dk = mm_t(bt, ck) * (0.5 * alive)
            dk = dk + jnp.transpose(dk)
            lower = pltpu.roll(dk[64:, :], 64, 1)
            dloc[3 * p + k, 0:64, :] = jnp.where((lane64 < 64) & (lane64 < row64), lower, dk[:64, :])
            tail = jnp.sum(jnp.where(lane64 == row64 + 64, dk[64:, :], 0.0), axis=0, keepdims=True)
            dloc[3 * p + k, 64:, :] = jnp.broadcast_to(tail, (8, FSZ))

    xl, xr = lax.rem(x + 3, 4), lax.rem(x + 1, 4)
    dcp = [
        remote(dloc.at[0:3], dpar.at[0:3], dsend.at[0], drecv.at[0], d, xl),
        remote(dloc.at[3:6], dpar.at[3:6], dsend.at[1], drecv.at[1], d, xr),
    ]
    for side, table in enumerate((to_next, to_prev)):
        for s in range(2):
            acc = table[s][0] * dloc[0]
            for k in range(1, 6):
                acc += table[s][k] * dloc[k]
            dsnd[side, s * PK : (s + 1) * PK, :] = acc
        slot = up_slot if side == 0 else lo_slot
        live = (slot < fc[0]).astype(F32)
        dsnd[side, 2 * PK :, :] = jnp.full((8, FSZ), 1.0, F32) * live
    for side, dd in enumerate((nxt, prv)):
        for q, xx in enumerate((x, (partner, beside)[side])):
            c = remote(
                dsnd.at[side], dnbr.at[side, e], dsend.at[2 + 2 * side + q],
                drecv.at[2 + 2 * side + e], dd, xx,
            )
            dcp.append(c)

    for c in dcp[2:] + dcp[:2]:
        c.start()

    sent = []

    def send_all(ex, t):
        tvec[ex] = t
        out = [remote(tvec.at[ex], rvec.at[ex], tsend.at[ex, 0], trecv.at[ex, 0], d, partner)]
        for side, table in enumerate((to_next, to_prev)):
            for s in range(2):
                acc = table[s][0] * t[:, face(0)]
                for k in range(1, 6):
                    acc += table[s][k] * t[:, face(k)]
                tnb[ex, side, s] = acc
            dd = (nxt, prv)[side]
            for q in range(2):
                c = remote(
                    tnb.at[ex, side], rnb.at[ex, side, e], tsend.at[ex, 1 + 2 * side + q],
                    trecv.at[ex, 1 + 2 * side + e], dd, 2 * h + q,
                )
                c.start()
                out.append(c)
        out[0].start()
        return out

    def settle(ex, cps):
        sent.extend(cps)
        remote(tvec.at[ex], rvec.at[ex], tsend.at[ex, 0], trecv.at[ex, 0], d, partner).wait_recv()
        for side in range(2):
            for q in range(2):
                remote(
                    tnb.at[ex, side], rnb.at[ex, side, q], tsend.at[ex, 0],
                    trecv.at[ex, 1 + 2 * side + q], d, partner,
                ).wait_recv()

    def assemble(ex, t, cps):
        settle(ex, cps)
        pv = [rnb[ex, 0, 0, s] + rnb[ex, 0, 1, s] for s in range(2)]
        nv = [rnb[ex, 1, 0, s] + rnb[ex, 1, 1, s] for s in range(2)]
        other = [rvec[ex, :, face(q)] for q in range(6)]
        cols = []
        for k in range(6):
            acc = t[:, face(k)]
            for q in range(6):
                acc += same[k][q] * other[q]
            acc += from_prev[k][0] * pv[0] + from_prev[k][1] * pv[1]
            acc += from_next[k][0] * nv[0] + from_next[k][1] * nv[1]
            cols.append(acc)
        return jnp.concatenate(cols, axis=1)

    lcopy.wait()
    loc[2].wait()
    srow = scal
    wgt = [
        (lown[...].astype(F32) * srow).astype(BF16).astype(F32),
        (lrecv[...].astype(F32) * srow).astype(BF16).astype(F32),
    ]
    low = e == 0
    weighted = jnp.concatenate(
        [jnp.where(low, wgt[0], wgt[1]), jnp.where(low, wgt[1], wgt[0])], axis=0
    ).astype(BF16)
    forced = mm(weighted, amat).astype(BF16)
    rloc = mm_t(forced, cmat[...]) * alive
    rcp = send_all(0, rloc)

    sent.extend(dcp)
    remote(dloc.at[0:3], dpar.at[0:3], dsend.at[0], drecv.at[0], d, partner).wait_recv()
    remote(dloc.at[3:6], dpar.at[3:6], dsend.at[0], drecv.at[1], d, partner).wait_recv()
    for side in range(2):
        for q in range(2):
            remote(
                dsnd.at[side], dnbr.at[side, q], dsend.at[0], drecv.at[2 + 2 * side + q], d, partner
            ).wait_recv()
    row = lax.broadcasted_iota(jnp.int32, (FSZ, FSZ), 0)
    col = lax.broadcasted_iota(jnp.int32, (FSZ, FSZ), 1)
    eye = (row == col).astype(F32)
    srows, scols = [], []
    for k in range(6):
        acc = dloc[k]
        for q in range(6):
            acc += same[k][q] * dpar[q]
        for s in range(2):
            at = slice(s * PK, (s + 1) * PK)
            acc += from_prev[k][s] * (dnbr[0, 0, at, :] + dnbr[0, 1, at, :])
            acc += from_next[k][s] * (dnbr[1, 0, at, :] + dnbr[1, 1, at, :])
        flag = jnp.full((1, FSZ), 1.0, F32) * (mine[k] < fc[0]).astype(F32)
        flag = jnp.where(mine[k] == NF, dnbr[0, 0, 2 * PK : 2 * PK + 1, :], flag)
        flag = jnp.where(mine[k] == NF + 1, dnbr[1, 0, 2 * PK : 2 * PK + 1, :], flag)
        body, tail = acc[:64, :], acc[64:65, :]
        keep = jnp.where(lane64 == row64, 0.5, 1.0)
        up = jnp.where(lane64 >= row64, body * keep, 0.0)
        dn = pltpu.roll(jnp.where(lane64 < row64, body, 0.0), 64, 1)
        dn = dn + jnp.where(lane64 == row64 + 64, 0.5 * tail, 0.0)
        half = jnp.concatenate([up, dn], axis=0)
        acc = half + jnp.transpose(half)
        acc = jnp.where(flag * alive > 0.5, acc, eye)
        diag = acc * eye
        srow_k = lax.rsqrt(jnp.sum(diag, axis=0, keepdims=True))
        scol_k = lax.rsqrt(jnp.sum(diag, axis=1, keepdims=True))
        srows.append(srow_k)
        scols.append(scol_k)
        msc[k * FSZ : (k + 1) * FSZ, :] = acc * srow_k * scol_k

    msc[6 * FSZ : 7 * FSZ, :] = eye
    msc[7 * FSZ :, :] = eye
    sub8 = lax.broadcasted_iota(jnp.int32, (8, FSZ), 0)
    lane8 = lax.broadcasted_iota(jnp.int32, (8, FSZ), 1)
    laneb = lax.broadcasted_iota(jnp.int32, (BL, FSZ), 1)
    rowb = lax.broadcasted_iota(jnp.int32, (BL, FSZ), 0)

    def at_lane(r, i):
        return jnp.broadcast_to(r[:, i : i + 1], (8, FSZ))

    def invert8(p):
        p = dict(p)

        def key(a, b):
            return (a, b) if a <= b else (b, a)

        for i in range(8):
            dinv_i = 1.0 / p[i, i]
            old = {a: p[key(a, i)] for a in range(8) if a != i}
            fac = {a: old[a] * dinv_i for a in old}
            for a in old:
                for b in old:
                    if a <= b:
                        p[a, b] = p[a, b] - fac[a] * old[b]
            for a in old:
                p[key(a, i)] = fac[a]
            p[i, i] = -dinv_i
        return {(a, b): p[key(a, b)] for a in range(8) for b in range(8)}

    for base in range(0, FSZ, BL):
        r = [msc[pl.ds(base + i, 8, stride=FSZ), :] for i in range(BL)]
        for lo in range(0, BL, 8):
            at = base + lo
            neg = invert8({
                (a, b): at_lane(r[lo + a], at + b) for a in range(8) for b in range(a, 8)
            })
            inside = (lane8 >= at) & (lane8 < at + 8)
            unit = [(lane8 == at + a).astype(F32) for a in range(8)]
            plain = [jnp.where(inside, -unit[b], r[lo + b]) for b in range(8)]
            y = []
            for a in range(8):
                acc = neg[a, 0] * plain[0]
                for b in range(1, 8):
                    acc += neg[a, b] * plain[b]
                y.append(acc)
            for i in range(lo + 8, BL):
                acc = jnp.where(inside, 0.0, r[i])
                for a in range(8):
                    acc += at_lane(r[i], at + a) * y[a]
                r[i] = acc
            for a in range(8):
                i = lo + a
                wrow[8 * i : 8 * i + 8, :] = r[i] - unit[a]
                zrow[8 * i : 8 * i + 8, :] = jnp.where(inside, unit[a], 0.0) - y[a]
        two = jnp.where(laneb == rowb + base, 2.0, 0.0)
        for k in range(6):
            xm = wrow[pl.ds(k, BL, stride=8), :]
            ym = zrow[pl.ds(k, BL, stride=8), :]
            x1 = xm.astype(BF16)
            x2 = (xm - x1.astype(F32)).astype(BF16)
            y1 = ym.astype(BF16)
            y2 = (ym - y1.astype(F32)).astype(BF16)
            xs = jnp.concatenate([x1, x1, x2], axis=0)
            ys = jnp.concatenate([y1, y2, y1], axis=0)
            upd = lax.dot_general(xs, ys, (((0,), (0,)), ((), ())), preferred_element_type=F32)
            mat = slice(k * FSZ, (k + 1) * FSZ)
            msc[mat, :] = msc[mat, :] - upd
            own_rows = slice(k * FSZ + base, k * FSZ + base + BL)
            msc[own_rows, :] = msc[own_rows, :] - two

    for k in range(6):
        di = -(msc[k * FSZ : (k + 1) * FSZ, :] * srows[k] * scols[k])
        hi = di.astype(BF16)
        dinv[k, :, 0:FSZ] = hi
        dinv[k, :, FSZ:] = (di - hi.astype(F32)).astype(BF16)

    def precondition(v):
        out = []
        for k in range(6):
            y = mm(parts(v[:, face(k)]), dinv[k])
            y = y[:NR] + y[NR:]
            out.append(y[:, :FSZ] + y[:, FSZ:])
        return jnp.concatenate(out, axis=1)

    def apply_s(v):
        u = mm(parts(v), btm[...])
        u = u[:NR] + u[NR:]
        t = mm_t(parts(u), cmat[...])
        return (t[:NR] + t[NR:]) * alive

    m0 = [sum(eq(n0[k], f) for k in range(6)) * al[0] for f in range(NF + 2)]
    m1 = [sum(eq(n1[k], f) for k in range(6)) * al[1] for f in range(NF + 2)]
    mine_w = [jnp.where(e == 0, al[0], al[1] * (1.0 - m0[f])) for f in range(NF + 2)]
    their_w = [jnp.where(e == 1, al[0], al[1] * (1.0 - m0[f])) for f in range(NF + 2)]

    def hand_on(v, w):
        vbuf[v] = w
        out = [
            remote(
                vbuf.at[v, pl.ds(pl.multiple_of(8 * oe, 8), 8), :], vpar.at[v], vsend.at[v, 0],
                vrecv.at[v, 0], d, partner,
            )
        ]
        for side, name in enumerate((NF + 1, NF)):
            acc = jnp.zeros((NR, FSZ), F32)
            for k in range(6):
                acc += (eq(mine[k], name) * mine_w[name]) * w[:, face(k)]
            vnb[side, v] = acc
            for q in range(2):
                out.append(
                    remote(
                        vnb.at[side, v, 8 * q : 8 * q + 8, :], vnbr.at[side, e, v],
                        vsend.at[v, 1 + 2 * side + q], vrecv.at[v, 1 + 2 * side + e],
                        (nxt, prv)[side], 2 * h + q,
                    )
                )
        for c in out:
            c.start()
        return out

    w = precondition(assemble(0, rloc, rcp))
    vcp = []
    for i in range(3):
        vcp += hand_on(i, w)
        t = apply_s(w)
        cps = send_all(1 + i, t)
        if i < 2:
            w = precondition(assemble(1 + i, t, cps)) - w

    def fold(v):
        acc = v[:, face(0)]
        for k in range(1, 6):
            acc += v[:, face(k)]
        return acc

    prods = []
    for i in range(3):
        wi = vbuf[i]
        for j in range(3):
            prods.append(fold(wi * tvec[1 + j]))
        prods.append(fold(wi * tvec[0]))
    pads = [jnp.zeros((NR, FSZ), F32)] * 4
    for c in range(2):
        stack = jnp.concatenate((prods + pads)[8 * c : 8 * c + 8], axis=0)
        pay[0, c : c + 1, :] = jnp.sum(jnp.transpose(stack), axis=0, keepdims=True)
    ra[me_a] = pay[0]

    def plane_send(o):
        dd, xx, s = plane_peer(o)
        return remote(pay.at[0], ra.at[me_a], asend.at[s], arecv.at[me_a], dd, xx)

    def plane_from(o):
        _dd, _xx, s = plane_peer(o)
        return remote(pay.at[0], ra.at[s], asend.at[s], arecv.at[s], d, partner)

    def axis_send(o):
        dd, xx, s = axis_peer(o)
        return remote(pay.at[1], rb.at[zz], bsend.at[s], brecv.at[zz], dd, xx)

    def axis_from(o):
        _dd, _xx, s = axis_peer(o)
        return remote(pay.at[1], rb.at[s], bsend.at[s], brecv.at[s], d, partner)

    @pl.loop(1, 2 * npl)
    def _(o):
        plane_send(o).start()

    @pl.loop(1, 2 * npl)
    def _(o):
        plane_from(o).wait_recv()

    tot = ra[0]
    for s in range(1, 2 * npl):
        tot = tot + ra[s]
    pay[1] = tot
    rb[zz] = tot

    @pl.loop(1, nz)
    def _(o):
        axis_send(o).start()

    settle(3, cps)
    sent.extend(vcp)
    for v in range(3):
        remote(vpar.at[v], vpar.at[v], vsend.at[0, 0], vrecv.at[v, 0], d, partner).wait_recv()
        for side in range(2):
            for q in range(2):
                remote(
                    vnb.at[side, v, 0:8, :], vnbr.at[side, q, v], vsend.at[0, 0],
                    vrecv.at[v, 1 + 2 * side + q], d, partner,
                ).wait_recv()
    rows = pl.ds(pl.multiple_of(8 * e, 8), 8)
    for f in range(NF):
        free = 1.0 - jnp.maximum(m0[f], m1[f])
        wp = free * eq(lo_slot, f) * has_prev
        wn = free * eq(up_slot, f) * has_next
        for v in range(3):
            acc = wp * (vnbr[0, 0, v] + vnbr[0, 1, v]) + wn * (vnbr[1, 0, v] + vnbr[1, 1, v])
            for k in range(6):
                acc += (eq(mine[k], f) * mine_w[f]) * vbuf[v, rows, face(k)]
                acc += (eq(theirs[k], f) * their_w[f]) * vpar[v, :, face(k)]
            outb[v, f] = acc
        tp = eq(lo_slot, f) * has_prev
        tn = eq(up_slot, f) * has_next
        for ex in range(4):
            acc = tp * (rnb[ex, 0, 0, 1, rows, :] + rnb[ex, 0, 1, 1, rows, :])
            acc += tn * (rnb[ex, 1, 0, 1, rows, :] + rnb[ex, 1, 1, 1, rows, :])
            for k in range(6):
                acc += eq(mine[k], f) * tvec[ex, rows, face(k)]
                acc += eq(theirs[k], f) * rvec[ex, rows, face(k)]
            outb[3 + ex, f] = acc

    @pl.loop(1, 2 * npl)
    def _(o):
        plane_send(o).wait_send()

    @pl.loop(1, nz)
    def _(o):
        axis_from(o).wait_recv()

    @pl.loop(1, nz)
    def _(o):
        axis_send(o).wait_send()

    for c in shards + sent:
        c.wait_send()
    tot = rb[0]
    for s in range(1, nz):
        tot = tot + rb[s]

    def pick(q):
        r = jnp.broadcast_to(tot[q // 8 : q // 8 + 1, :], (8, FSZ))
        at = (q % 8) * NR + 8 * e
        return jnp.sum(jnp.where(lane8 == sub8 + at, r, 0.0), axis=1, keepdims=True)

    g = [[pick(4 * i + j) for j in range(3)] for i in range(3)]
    gr = [pick(4 * i + 3) for i in range(3)]

    zero = jnp.zeros((8, 1), F32)
    pi = [zero + 1.0, zero, zero]
    rho = [zero, zero, zero]
    xc = [zero, zero, zero]
    rz = gr[0]
    for it in range(3):
        psp = zero
        for i in range(it + 1):
            for j in range(it + 1):
                psp += pi[i] * pi[j] * g[i][j]
        alpha = rz / psp
        xc = [xc[i] + alpha * pi[i] for i in range(3)]
        rho = [rho[i] - alpha * pi[i] for i in range(3)]
        if it == 2:
            break
        zc = [1.0 + rho[0], rho[0] + rho[1], rho[1] + rho[2]]
        new = zero
        for i in range(it + 2):
            s = gr[i]
            for j in range(it + 1):
                s += rho[j] * g[i][j]
            new += zc[i] * s
        beta = new / rz
        pi = [zc[i] + beta * pi[i] for i in range(3)]
        rz = new
    xb = [jnp.broadcast_to(c, (8, FSZ)) for c in xc]
    rbc = [jnp.broadcast_to(c, (8, FSZ)) for c in rho]
    for f in range(NF):
        sol[f] = xb[0] * outb[0, f] + xb[1] * outb[1, f] + xb[2] * outb[2, f]
        res[f] = outb[3, f] + rbc[0] * outb[4, f] + rbc[1] * outb[5, f] + rbc[2] * outb[6, f]


def per_device(nd, npl, elem_count, face_count, bound_slot, elem_face, density, coupling, ainv, loads):
    columns = jnp.swapaxes(coupling, 1, 2)
    smem = pl.BlockSpec(memory_space=pltpu.SMEM)
    vmem = pl.BlockSpec(memory_space=pltpu.VMEM)
    hbm = pl.BlockSpec(memory_space=pltpu.HBM)
    dma = pltpu.SemaphoreType.DMA
    nz = nd // npl
    out = pltpu.VMEM((NF, 8, FSZ), F32)
    vm = pltpu.VMEM
    return pl.pallas_call(
        functools.partial(kernel, nd, npl),
        out_shape=(out, out),
        in_specs=[smem, smem] + [hbm] * 6,
        out_specs=(vmem, vmem),
        scratch_shapes=[
            pltpu.SMEM((1, 2), jnp.int32),
            pltpu.SMEM((2, 6), jnp.int32),
            vm((TR, TR), BF16),
            vm((TR, TR), BF16),
            vm((TR, TR), BF16),
            vm((TR, TR), BF16),
            vm((2, TR), F32),
            vm((8, TR), BF16),
            vm((8, TR), BF16),
            vm((6, PK, FSZ), F32),
            vm((6, PK, FSZ), F32),
            vm((2, 2 * PK + 8, FSZ), F32),
            vm((2, 2, 2 * PK + 8, FSZ), F32),
            vm((8 * FSZ, FSZ), F32),
            vm((8 * BL, FSZ), F32),
            vm((8 * BL, FSZ), F32),
            vm((6, FSZ, 2 * FSZ), BF16),
            vm((4, NR, TR), F32),
            vm((4, 2, 2, NR, FSZ), F32),
            vm((4, NR, TR), F32),
            vm((4, 2, 2, 2, NR, FSZ), F32),
            vm((3, NR, TR), F32),
            vm((3, 8, TR), F32),
            vm((2, 3, NR, FSZ), F32),
            vm((2, 2, 3, 8, FSZ), F32),
            vm((7, NF, 8, FSZ), F32),
            vm((2, 2, FSZ), F32),
            vm((2 * npl, 2, FSZ), F32),
            vm((nz, 2, FSZ), F32),
            pltpu.SemaphoreType.REGULAR((2,)),
            dma((6,)), dma((3,)), dma((4,)), dma, dma, dma((6,)), dma((6,)),
            dma((4, 5)), dma((4, 5)), dma((3, 5)), dma((3, 5)),
            dma((2 * npl,)), dma((2 * npl,)), dma((nz,)), dma((nz,)),
        ],
        compiler_params=pltpu.CompilerParams(
            collective_id=0, has_side_effects=True, vmem_limit_bytes=VMEM_ALL
        ),
        name="condense_cg",
    )(elem_count, face_count, bound_slot, elem_face, density, columns, loads, ainv)


def solution(mesh):
    placed = (
        P("dom"),
        P("dom"),
        P("dom", None),
        P("dom", None),
        P("dom", None),
        P("dom", None, "rhs"),
        P(),
        P("dom", "rhs", None),
    )
    nd = mesh.shape["dom"]
    npl = min(PLANE, nd // 2)
    return jax.shard_map(
        functools.partial(per_device, nd, npl),
        mesh=mesh,
        in_specs=placed,
        out_specs=(P("dom", "rhs", None), P("dom", "rhs", None)),
        check_vma=False,
    )
```
